256 devices in a mesh: row: 32 (over z, y_hi, core), col: 8 (over x, y_lo).
Axes of the slice: x: 4, y: 4 (y_hi: 2, y_lo: 2; y = y_hi * 2 + y_lo), z: 8, core: 2. Of those that a mesh axis runs over, the one named last changes fastest.
Arguments:
- feature_map: bfloat16 [256, 256, 384], P('row', 'col'), may hold values from -6 to 6
- kernel: float32 [7, 7, 384], replicated, may hold values from -0.875 to 0.875
- ln_gain: float32 [384], replicated, may hold values from 0.5 to 1.5
- ln_bias: float32 [384], replicated, may hold values from -3 to 3
- w_in: bfloat16 [384, 1536], P(None, ('row', 'col')), may hold values from -0.3125 to 0.3125
- b_in: float32 [1536], replicated, may hold values from -3 to 3
- w_out: bfloat16 [1536, 384], P(('row', 'col')), may hold values from -0.15625 to 0.15625
- b_out: float32 [384], replicated, may hold values from -3 to 3
- layer_scale: float32 [384], replicated, may hold values from 0.5 to 1.5
- cotangent: bfloat16 [256, 256, 384], P('row', 'col'), may hold values from -6 to 6
Outputs:
- block_out: bfloat16 [256, 256, 384], P('row', 'col')
- grad_input: bfloat16 [256, 256, 384], P('row', 'col')
- grad_w_in: float32 [384, 1536], P(None, ('row', 'col'))
- grad_w_out: float32 [1536, 384], P(('row', 'col'))
- small_grads: float32 [53, 384], replicated
- grad_b_in: float32 [1536], replicated
The draws below stay inside these ranges and needn't reach their ends.
All inputs are finite; a program needn't handle non-finite values.
Results may differ from the reference program's by a relative error of at most 0.007.
Values may be sent and summed in bfloat16 or wider, within the bound.
No kernel may reach another device: no remote copies, remote signals or barrier semaphores. Data moves between devices by JAX's collectives and lax.ppermute only.
A program may use at most 64 MiB of HBM per device.

```python
import math
import jax
import jax.numpy as jnp
from jax import lax

C = 384
HID = 1536
KS = 7
HEIGHT = 256
WIDTH = 256


def shard_levels(stream_key, extent, cuts, low, high):
    loudness, own = 1.0, jax.random.fold_in(stream_key, 6)
    for axis_at, blocks in cuts:
        draws = jnp.exp(jax.random.uniform(jax.random.fold_in(own, axis_at), (blocks,), jnp.float32, low / len(cuts), high / len(cuts)))
        loudness = loudness * jnp.repeat(draws, extent[axis_at] // blocks).reshape([-1 if axis == axis_at else 1 for axis in range(len(extent))])
    return loudness


def scatter_about(key, shape, spread, bound, pieces=(), dtype=jnp.bfloat16):
    array = spread * jax.random.normal(key, shape, jnp.float32)
    if pieces:
        array = array * shard_levels(key, shape, pieces, -0.22, 0.18)
    return jnp.clip(array, -bound, bound).astype(dtype)


def setup_inputs(seed: int = 0) -> dict:
    arg_keys = jax.random.split(jax.random.key(seed), 11)
    feature_map = scatter_about(arg_keys[0], (HEIGHT, WIDTH, C), 1.0, 6.0, ((0, 32), (1, 8)))
    kernel = scatter_about(arg_keys[1], (KS, KS, C), (KS * KS) ** -0.5, 0.875, (), jnp.float32)
    ln_gain = jnp.clip(1.0 + 0.1 * jax.random.normal(arg_keys[2], (C,), jnp.float32), 0.5, 1.5)
    ln_bias = scatter_about(arg_keys[3], (C,), 0.5, 3.0, (), jnp.float32)
    w_in = scatter_about(arg_keys[4], (C, HID), C ** -0.5, 0.3125, ((1, 256),))
    b_in = scatter_about(arg_keys[5], (HID,), 0.5, 3.0, (), jnp.float32)
    w_out = scatter_about(arg_keys[6], (HID, C), HID ** -0.5, 0.15625, ((0, 256),))
    b_out = scatter_about(arg_keys[7], (C,), 0.5, 3.0, (), jnp.float32)
    layer_scale = jnp.clip(1.0 + 0.1 * jax.random.normal(arg_keys[8], (C,), jnp.float32), 0.5, 1.5)
    cotangent = scatter_about(arg_keys[9], (HEIGHT, WIDTH, C), 1.0, 6.0, ((0, 32), (1, 8)))
    return dict(feature_map=feature_map, kernel=kernel, ln_gain=ln_gain, ln_bias=ln_bias, w_in=w_in, b_in=b_in, w_out=w_out, b_out=b_out, layer_scale=layer_scale, cotangent=cotangent)


def gelu_parts(hidden):
    normal_cdf = 0.5 * (1.0 + jax.scipy.special.erf(hidden * (1.0 / math.sqrt(2.0))))
    density = jnp.exp(-0.5 * hidden * hidden) * (1.0 / math.sqrt(2.0 * math.pi))
    return (hidden * normal_cdf, normal_cdf + hidden * density)

def depthwise(padded, kernel, height, width):
    result = jnp.zeros((height, width, padded.shape[2]), jnp.float32)
    for tap_row in range(7):
        for tap_col in range(7):
            result = result + padded[tap_row:tap_row + height, tap_col:tap_col + width] * kernel[tap_row, tap_col]
    return result

def reference(feature_map, kernel, ln_gain, ln_bias, w_in, b_in, w_out, b_out, layer_scale, cotangent):
    height, width, channels = feature_map.shape
    source = feature_map.astype(jnp.float32)
    padded = jnp.pad(source, ((3, 3), (3, 3), (0, 0)))
    conv = depthwise(padded, kernel, height, width)
    average = lax.optimization_barrier(jnp.mean(conv, -1, keepdims=True))
    centered = conv - average
    variance = lax.optimization_barrier(jnp.mean(centered * centered, -1, keepdims=True))
    inv_std = lax.rsqrt(variance + 1e-06)
    unit_scaled = centered * inv_std
    normed = (unit_scaled * ln_gain + ln_bias).astype(jnp.bfloat16)

    def row_step(carry, inputs):
        acc_win, acc_wout, acc_bin, acc_bout, acc_scale = carry
        normed_row, source_row, cot_row = inputs
        hidden = jnp.dot(normed_row, w_in, preferred_element_type=jnp.float32) + b_in
        act_value, slope = gelu_parts(hidden)
        activated = act_value.astype(jnp.bfloat16)
        mixed = jnp.dot(activated, w_out, preferred_element_type=jnp.float32) + b_out
        out_row = (source_row.astype(jnp.float32) + layer_scale * mixed).astype(jnp.bfloat16)
        grad_flow = cot_row.astype(jnp.float32)
        grad_mixed = grad_flow * layer_scale
        mixed_low = grad_mixed.astype(jnp.bfloat16)
        acc_wout = acc_wout + jnp.dot(activated.T, mixed_low, preferred_element_type=jnp.float32)
        grad_act = jnp.dot(mixed_low, w_out.T, preferred_element_type=jnp.float32)
        grad_hidden = (grad_act * slope).astype(jnp.bfloat16)
        acc_win = acc_win + jnp.dot(normed_row.T, grad_hidden, preferred_element_type=jnp.float32)
        acc_bin = acc_bin + lax.optimization_barrier(jnp.sum(grad_hidden.astype(jnp.float32), 0))
        acc_bout = acc_bout + lax.optimization_barrier(jnp.sum(grad_mixed, 0))
        acc_scale = acc_scale + lax.optimization_barrier(jnp.sum(grad_flow * mixed, 0))
        grad_normed = jnp.dot(grad_hidden, w_in.T, preferred_element_type=jnp.float32)
        return ((acc_win, acc_wout, acc_bin, acc_bout, acc_scale), (out_row, grad_normed))
    hidden_count = w_in.shape[1]
    start_carry = (jnp.zeros((channels, hidden_count), jnp.float32), jnp.zeros((hidden_count, channels), jnp.float32), jnp.zeros((hidden_count,), jnp.float32), jnp.zeros((channels,), jnp.float32), jnp.zeros((channels,), jnp.float32))
    sums, outputs = lax.scan(row_step, start_carry, (normed, feature_map, cotangent))
    grad_win, grad_wout, grad_bin, grad_bout, grad_scale = sums
    block_out, grad_normed = outputs
    grad_gain = lax.optimization_barrier(jnp.sum(grad_normed * unit_scaled, (0, 1)))
    grad_lnb = lax.optimization_barrier(jnp.sum(grad_normed, (0, 1)))
    scaled_grad = grad_normed * ln_gain
    grad_conv = inv_std * (scaled_grad - lax.optimization_barrier(jnp.mean(scaled_grad, -1, keepdims=True)) - unit_scaled * lax.optimization_barrier(jnp.mean(scaled_grad * unit_scaled, -1, keepdims=True)))
    tap_terms = []
    for tap_row in range(7):
        for tap_col in range(7):
            tap_terms.append(lax.optimization_barrier(jnp.sum(padded[tap_row:tap_row + height, tap_col:tap_col + width] * grad_conv, (0, 1))))
    grad_low = grad_conv.astype(jnp.bfloat16)
    grad_pad = jnp.pad(grad_low.astype(jnp.float32), ((3, 3), (3, 3), (0, 0)))
    back_conv = jnp.zeros((height, width, channels), jnp.float32)
    for tap_row in range(7):
        for tap_col in range(7):
            back_conv = back_conv + grad_pad[6 - tap_row:6 - tap_row + height, 6 - tap_col:6 - tap_col + width] * kernel[tap_row, tap_col]
    grad_input = (cotangent.astype(jnp.float32) + back_conv).astype(jnp.bfloat16)
    small_grads = jnp.concatenate([jnp.stack(tap_terms, 0), grad_gain[None], grad_lnb[None], grad_bout[None], grad_scale[None]], 0)
    return (block_out, grad_input, grad_win, grad_wout, small_grads, grad_bin)
```

```python
import math

import jax
import jax.numpy as jnp
from jax import lax
from jax.sharding import Mesh
from jax.sharding import PartitionSpec as P

ROW = ("z", "yh", "c")
COL = ("x", "yl")
Y = ("yh", "yl")
BF = jnp.bfloat16
F4 = jnp.float32


def swap(x, axis, flip):
    count = lax.axis_size(axis)
    return lax.ppermute(x, axis, [(i, i ^ flip) for i in range(count)])


def padded_2(x, sides, width):
    for axis, dim in sides:
        peers, length = (lax.axis_size(axis), x.shape[dim])
        up = [(i, (i + 1) % peers) for i in range(peers - 1)]
        down = [(j, i) for i, j in up]
        last = lax.slice_in_dim(x, length - width, length, axis=dim)
        first = lax.slice_in_dim(x, 0, width, axis=dim)
        before = lax.ppermute(last, axis, up)
        after = lax.ppermute(first, axis, down)
        x = jnp.concatenate([before, x, after], axis=dim)
    return x


def gelu_parts(hidden):
    normal_cdf = 0.5 * (1.0 + jax.scipy.special.erf(hidden * (1.0 / math.sqrt(2.0))))
    density = jnp.exp(-0.5 * hidden * hidden) * (1.0 / math.sqrt(2.0 * math.pi))
    return (hidden * normal_cdf, normal_cdf + hidden * density)


def extend(field):
    return padded_2(field, ((ROW, 0), (COL, 1)), 3)


def pair_gather(x, axis, bit):
    mine = (lax.axis_index(axis) & bit) != 0
    other = swap(x, axis, bit)
    return jnp.concatenate([jnp.where(mine, other, x), jnp.where(mine, x, other)], axis=1)


def quad_gather(x, axis):
    me = lax.axis_index(axis)
    rows = x.shape[1]
    others = [swap(x, axis, flip) for flip in (1, 2, 3)]
    full = jnp.zeros((x.shape[0], 4 * rows, x.shape[2]), x.dtype)
    for flip, piece in zip((0, 1, 2, 3), [x] + others):
        full = lax.dynamic_update_slice_in_dim(full, piece, (me ^ flip) * rows, axis=1)
    return full


def piece_of(x, index, rows):
    return lax.dynamic_slice_in_dim(x, index * rows, rows, axis=1)


def fan_reduce(x, axis, flips, size, dtype):
    rows = x.shape[1] // size
    where = lax.axis_index(axis)
    unit = flips[0]
    me = (where // unit) % size
    total = piece_of(x, me, rows)
    got = [swap(piece_of(x, me ^ (flip // unit), rows).astype(dtype), axis, flip) for flip in flips]
    for g in got:
        total = total + g.astype(F4)
    return total


def on_device(
    feature_map, kernel, ln_gain, ln_bias, w_in, b_in, w_out, b_out, layer_scale, cotangent
):
    row_count, col_count, channels = feature_map.shape
    pixels = row_count * col_count
    hidden_count = b_in.shape[0]
    contract_last = (((1,), (1,)), ((), ()))
    contract_first = (((0,), (0,)), ((), ()))

    weights = jnp.stack([w_in.T, w_out], 0)
    for bit in (4, 2, 1):
        weights = pair_gather(weights, "z", bit)
    weights = quad_gather(weights, Y)
    weights = quad_gather(weights, "x")
    weights = pair_gather(weights, "c", 1)
    w_in_t, w_out_full = weights[0], weights[1]
    units = hidden_count // 256
    b_mine = (
        b_in.reshape(2, 2, 2, 2, 2, 4, 2, units).transpose(4, 5, 3, 6, 2, 1, 0, 7).reshape(hidden_count)
    )

    padded = extend(feature_map).astype(F4)
    conv = jnp.zeros((row_count, col_count, channels), F4)
    for tap_row in range(7):
        for tap_col in range(7):
            conv = (
                conv
                + padded[tap_row : tap_row + row_count, tap_col : tap_col + col_count]
                * kernel[tap_row, tap_col]
            )
    average = jnp.mean(conv, -1, keepdims=True)
    centered = conv - average
    variance = jnp.mean(centered * centered, -1, keepdims=True)
    inv_std = lax.rsqrt(variance + 1e-06)
    unit_scaled = centered * inv_std
    normed = (unit_scaled * ln_gain + ln_bias).astype(BF).reshape(pixels, channels)
    hidden = lax.dot_general(normed, w_in_t, contract_last, preferred_element_type=F4) + b_mine
    act_value, slope = gelu_parts(hidden)
    activated = act_value.astype(BF)
    mixed = jnp.dot(activated, w_out_full, preferred_element_type=F4) + b_out
    source = feature_map.astype(F4).reshape(pixels, channels)
    block_out = (source + layer_scale * mixed).astype(BF).reshape(row_count, col_count, channels)
    grad_flow = cotangent.astype(F4).reshape(pixels, channels)
    grad_mixed = grad_flow * layer_scale
    mixed_low = grad_mixed.astype(BF)
    grad_act = lax.dot_general(mixed_low, w_out_full, contract_last, preferred_element_type=F4)
    grad_hidden = (grad_act * slope).astype(BF)
    wout_term = lax.dot_general(activated, mixed_low, contract_first, preferred_element_type=F4)
    win_term = lax.dot_general(grad_hidden, normed, contract_first, preferred_element_type=F4)

    terms = jnp.stack([win_term, wout_term], 0)
    terms = fan_reduce(terms, "c", (1,), 2, BF)
    terms = fan_reduce(terms, "x", (1, 2, 3), 4, BF)
    terms = fan_reduce(terms, Y, (1, 2, 3), 4, BF)
    for bit in (1, 2, 4):
        terms = fan_reduce(terms, "z", (bit,), 2, F4)
    grad_w_in, grad_w_out = terms[0].T, terms[1]

    grad_normed = jnp.dot(grad_hidden, w_in_t, preferred_element_type=F4)
    grad_normed = grad_normed.reshape(row_count, col_count, channels)
    grad_gain = jnp.sum(grad_normed * unit_scaled, (0, 1))
    grad_lnb = jnp.sum(grad_normed, (0, 1))
    scaled_grad = grad_normed * ln_gain
    grad_conv = inv_std * (
        scaled_grad
        - jnp.mean(scaled_grad, -1, keepdims=True)
        - unit_scaled * jnp.mean(scaled_grad * unit_scaled, -1, keepdims=True)
    )
    tap_terms = []
    for tap_row in range(7):
        for tap_col in range(7):
            tap_terms.append(
                jnp.sum(
                    padded[tap_row : tap_row + row_count, tap_col : tap_col + col_count]
                    * grad_conv,
                    (0, 1),
                )
            )
    grad_pad = extend(grad_conv.astype(BF)).astype(F4)
    back_conv = jnp.zeros((row_count, col_count, channels), F4)
    for tap_row in range(7):
        for tap_col in range(7):
            back_conv = (
                back_conv
                + grad_pad[
                    6 - tap_row : 6 - tap_row + row_count, 6 - tap_col : 6 - tap_col + col_count
                ]
                * kernel[tap_row, tap_col]
            )
    grad_input = (cotangent.astype(F4) + back_conv).astype(BF)
    bias_local = jnp.sum(grad_hidden.astype(F4), 0)
    bias_local = (
        bias_local.reshape(2, 4, 2, 2, 2, 2, 2, units)
        .transpose(6, 5, 4, 2, 0, 1, 3, 7)
        .reshape(hidden_count // channels, channels)
    )
    small = jnp.concatenate(
        [
            jnp.stack(tap_terms, 0),
            grad_gain[None],
            grad_lnb[None],
            jnp.sum(grad_mixed, 0)[None],
            jnp.sum(grad_flow * mixed, 0)[None],
            bias_local,
        ],
        0,
    )
    for axis, bits in (("c", (1,)), ("x", (1, 2)), (Y, (1, 2)), ("z", (1, 2, 4))):
        for bit in bits:
            small = small + swap(small, axis, bit)
    return (block_out, grad_input, grad_w_in, grad_w_out, small[:53], small[53:].reshape(hidden_count))


def solution(mesh):
    fine = Mesh(mesh.devices.reshape(8, 2, 2, 4, 2), ("z", "yh", "c", "x", "yl"))
    every = ROW + COL
    placed = (
        P(ROW, COL, None),
        P(),
        P(),
        P(),
        P(None, every),
        P(),
        P(every, None),
        P(),
        P(),
        P(ROW, COL, None),
    )
    return jax.shard_map(
        on_device,
        mesh=fine,
        in_specs=placed,
        out_specs=(
            P(ROW, COL, None),
            P(ROW, COL, None),
            P(None, every),
            P(every, None),
            P(),
            P(),
        ),
        check_vma=False,
    )
```

```python
import functools
import math

import jax
import jax.numpy as jnp
from jax import lax
from jax.experimental import pallas as pl
from jax.experimental.pallas import tpu as pltpu
from jax.sharding import Mesh
from jax.sharding import PartitionSpec as P

ROW = ("z", "yh", "c")
COL = ("x", "yl")
Y = ("yh", "yl")
BF = jnp.bfloat16
F4 = jnp.float32


def swap(x, axis, flip):
    count = lax.axis_size(axis)
    return lax.ppermute(x, axis, [(i, i ^ flip) for i in range(count)])


def edge_sends(x, axis, dim, width=3):
    length = x.shape[dim]
    odd = (lax.axis_index(axis) & 1) != 0
    last = lax.slice_in_dim(x, length - width, length, axis=dim)
    first = lax.slice_in_dim(x, 0, width, axis=dim)
    return jnp.where(odd, first, last), jnp.where(odd, last, first)


def outer_swap(x, axis):
    peers = lax.axis_size(axis)
    return lax.ppermute(x, axis, [(i, ((i + 1) ^ 1) - 1) for i in range(1, peers - 1)])


def edge_order(inner, outer, axis):
    odd = (lax.axis_index(axis) & 1) != 0
    return jnp.where(odd, inner, outer), jnp.where(odd, outer, inner)


def edges(x, axis, dim):
    inner, outer = edge_sends(x, axis, dim)
    return edge_order(swap(inner, axis, 1), outer_swap(outer, axis), axis)


def between(x, sides, dim):
    return jnp.concatenate([sides[0], x, sides[1]], axis=dim)


def gelu_parts(hidden):
    normal_cdf = 0.5 * (1.0 + jax.scipy.special.erf(hidden * (1.0 / math.sqrt(2.0))))
    density = jnp.exp(-0.5 * hidden * hidden) * (1.0 / math.sqrt(2.0 * math.pi))
    return (hidden * normal_cdf, normal_cdf + hidden * density)


def pair_gather(x, axis, bit):
    mine = (lax.axis_index(axis) & bit) != 0
    other = swap(x, axis, bit)
    return jnp.concatenate([jnp.where(mine, other, x), jnp.where(mine, x, other)], axis=1)


def quad_select(x, axis, unit):
    me = (lax.axis_index(axis) // unit) % 4
    parts = [x] + [swap(x, axis, flip * unit) for flip in (1, 2, 3)]
    low, high = (me & 1) != 0, (me & 2) != 0
    pairs = [(parts[0], parts[1]), (parts[2], parts[3])]
    ordered = [(jnp.where(low, q, p), jnp.where(low, p, q)) for p, q in pairs]
    first, second = ordered
    low_half = [jnp.where(high, q, p) for p, q in zip(first, second)]
    high_half = [jnp.where(high, p, q) for p, q in zip(first, second)]
    return jnp.concatenate(low_half + high_half, axis=1)


def quad_gather(x, axis, extra=None):
    me = lax.axis_index(axis)
    rows, channels = x.shape[1:]
    others = []
    for flip in (1, 2, 3):
        if flip == 1 and extra is not None:
            got = swap(jnp.concatenate([x.reshape(2 * rows, channels), extra], 0), axis, flip)
            others.append(got[: 2 * rows].reshape(x.shape))
            extra = got[2 * rows :]
        else:
            others.append(swap(x, axis, flip))
    full = jnp.zeros((x.shape[0], 4 * rows, channels), x.dtype)
    for flip, piece in zip((0, 1, 2, 3), [x] + others):
        full = lax.dynamic_update_slice_in_dim(full, piece, (me ^ flip) * rows, axis=1)
    return full if extra is None else (full, extra)


def local_call(kernel, index, outs, *arrays, scratch=(), flops=1_000_000):
    moved = sum(math.prod(a.shape) * a.dtype.itemsize for a in list(arrays) + list(outs))
    return pl.pallas_call(
        kernel,
        out_shape=outs,
        in_specs=[pl.BlockSpec(memory_space=pltpu.SMEM)]
        + [pl.BlockSpec(memory_space=pltpu.VMEM)] * len(arrays),
        out_specs=[pl.BlockSpec(memory_space=pltpu.VMEM)] * len(outs),
        scratch_shapes=list(scratch),
        cost_estimate=pl.CostEstimate(flops=flops, bytes_accessed=moved, transcendentals=0),
        compiler_params=pltpu.CompilerParams(vmem_limit_bytes=32 * 2**20),
    )(index, *arrays)


def shape(*dims, dtype=F4):
    return jax.ShapeDtypeStruct(dims, dtype)


SMALL = 64


def norm_back(
    index, normed_grad, mixed, back, conv, gain, padded, cot, feature, scale, b_out, bias,
    low, message, outer, block_out, grads, wide, sums,
):
    rows, cols, channels = low.shape
    pixels = rows * cols

    def flat(x):
        return x.reshape(pixels, channels)

    taken = flat(conv[...])
    centered = taken - jnp.mean(taken, -1, keepdims=True)
    inv_std = lax.rsqrt(jnp.mean(centered * centered, -1, keepdims=True) + 1e-06)
    unit = centered * inv_std
    grad = normed_grad[0:pixels, :] + back[1].astype(F4)
    scaled = grad * gain[...]
    grad_conv = inv_std * (
        scaled
        - jnp.mean(scaled, -1, keepdims=True)
        - unit * jnp.mean(scaled * unit, -1, keepdims=True)
    )
    grads[...] = grad_conv.reshape(rows, cols, channels)
    low[...] = grad_conv.reshape(rows, cols, channels).astype(BF)
    sums[...] = jnp.zeros_like(sums)
    sums[49:50, :] = jnp.sum(grad * unit, 0, keepdims=True)
    sums[50:51, :] = jnp.sum(grad, 0, keepdims=True)
    full = mixed[0:pixels, :] + back[0].astype(F4) + b_out[...]
    flow = flat(cot[...].astype(F4))
    sums[51:52, :] = jnp.sum(flow * scale[...], 0, keepdims=True)
    sums[52:53, :] = jnp.sum(flow * full, 0, keepdims=True)
    sums[53:57, :] = bias[...]
    block_out[...] = (
        (flat(feature[...].astype(F4)) + scale[...] * full).astype(BF).reshape(rows, cols, channels)
    )
    for r in range(rows + 6):
        wide[r, 0 : cols + 6, :] = padded[r].astype(F4)
    for j in range(7):
        total = [jnp.zeros((8, channels), F4) for _ in range(7)]
        for r in range(rows + 6):
            slab = wide[r, j : j + cols, :]
            for p in range(max(0, r - 6), min(rows, r + 1)):
                term = slab * grads[p]
                term = tree([term[8 * k : 8 * k + 8] for k in range(cols // 8)])
                total[r - p] = total[r - p] + term
        for i in range(7):
            sums[7 * i + j : 7 * i + j + 1, :] = jnp.sum(total[i], 0, keepdims=True)
    message[0:SMALL, :] = sums[...].astype(BF)
    odd = index[0] != 0
    first, last = grads[0:3], grads[rows - 3 : rows]
    message[SMALL : SMALL + 3 * cols, :] = (
        jnp.where(odd, first, last).astype(BF).reshape(3 * cols, channels)
    )
    outer[...] = jnp.where(odd, last, first).astype(BF)


def first_fan(index, win, wout, mine, theirs, one, two, three, shared):
    rows = win.shape[0] // 4
    shared[...] = (mine[0:SMALL, :].astype(F4) + theirs[0:SMALL, :].astype(F4)).astype(BF)
    for flip, message in ((1, one), (2, two), (3, three)):
        at = pl.multiple_of((index[1] ^ flip) * rows, rows)
        message[0:rows, :] = win[pl.ds(at, rows), :].astype(BF)
        message[rows : 2 * rows, :] = wout[pl.ds(at, rows), :].astype(BF)
        message[2 * rows :, :] = shared[...]


def second_fan(index, win, wout, mine, g1, g2, g3, total, one, two, three, shared):
    rows = win.shape[0] // 4
    at = pl.multiple_of(index[1] * rows, rows)
    for k, term in enumerate((win, wout)):
        own = term[pl.ds(at, rows), :]
        got = [g[k * rows : (k + 1) * rows, :].astype(F4) for g in (g1, g2, g3)]
        total[k] = tree([own] + got)
    small = tree([mine[...].astype(F4)] + [g[2 * rows :, :].astype(F4) for g in (g1, g2, g3)])
    shared[...] = small.astype(BF)
    part = rows // 4
    for flip, message in ((1, one), (2, two), (3, three)):
        at = pl.multiple_of((index[2] ^ flip) * part, part)
        for k in range(2):
            message[k * part : (k + 1) * part, :] = total[k, pl.ds(at, part), :].astype(BF)
        message[2 * part :, :] = shared[...]


def up16(n):
    return -(-n // 16) * 16


def send_half(total, k, bit, message):
    half = total.shape[1] // 2
    block = up16(half)
    value = jnp.where(bit, total[k, 0:half, :], total[k, half : 2 * half, :])
    message[k * block : k * block + half, :] = value.astype(BF)


def third_fan(index, before, mine, g1, g2, g3, total, message, shared):
    rows = before.shape[1] // 4
    at = pl.multiple_of(index[2] * rows, rows)
    for k in range(2):
        got = [g[k * rows : (k + 1) * rows, :].astype(F4) for g in (g1, g2, g3)]
        total[k] = tree([before[k, pl.ds(at, rows), :]] + got)
    small = tree([mine[...].astype(F4)] + [g[2 * rows :, :].astype(F4) for g in (g1, g2, g3)])
    shared[...] = small.astype(BF)
    held = message.shape[0] - SMALL
    for k in range(2):
        send_half(total, k, index[3] != 0, message)
    message[held:, :] = shared[...]


def pair_step(here, after, index, before, mine, got, total, message, shared):
    half = before.shape[1] // 2
    block = up16(half)
    bit = index[here] != 0
    for k in range(2):
        own = jnp.where(bit, before[k, half : 2 * half, :], before[k, 0:half, :])
        total[k] = own + got[k * block : k * block + half, :].astype(F4)
    shared[...] = (mine[...].astype(F4) + got[2 * block :, :].astype(F4)).astype(BF)
    for k in range(2):
        send_half(total, k, index[after] != 0, message)
    message[message.shape[0] - SMALL :, :] = shared[...]


def pair_end(here, index, before, mine, got, win, wout, small, bias):
    half = before.shape[1] // 2
    block = up16(half)
    bit = index[here] != 0
    for k, out in ((0, win), (1, wout)):
        own = jnp.where(bit, before[k, half : 2 * half, :], before[k, 0:half, :])
        out[...] = own + got[k * block : k * block + half, :].astype(F4)
    total = mine[...].astype(F4) + got[2 * block :, :].astype(F4)
    small[...] = total[0:53, :]
    bias[...] = total[53:57, :]


def tree(parts):
    while len(parts) > 1:
        parts = [p + q for p, q in zip(parts[::2], parts[1::2])]
    return parts[0]


def on_device(
    feature_map, kernel, ln_gain, ln_bias, w_in, b_in, w_out, b_out, layer_scale, cotangent
):
    row_count, col_count, channels = feature_map.shape
    pixels = row_count * col_count
    hidden_count = b_in.shape[0]
    contract_last = (((1,), (1,)), ((), ()))
    contract_first = (((0,), (0,)), ((), ()))

    weights = jnp.stack([w_in.T, w_out], 0)
    weights = quad_select(weights, "z", 2)
    weights = pair_gather(weights, "z", 1)
    rows = edges(feature_map, ROW, 0)
    weights, feature_map, cotangent, rows = lax.optimization_barrier(
        (weights, feature_map, cotangent, rows)
    )
    tall = between(feature_map, rows, 0)
    inner, outer = edge_sends(tall, COL, 1)
    outer_got = outer_swap(outer, COL)
    weights, inner_got = quad_gather(weights, Y, inner.reshape(-1, channels))
    columns = edge_order(inner_got.reshape(inner.shape), outer_got, COL)
    weights, tall, columns, cotangent, kernel = lax.optimization_barrier(
        (weights, tall, columns, cotangent, kernel)
    )
    weights = quad_gather(weights, "x")
    w_in_t, w_out_mine = weights[0], weights[1]
    core = lax.axis_index("c")
    half = hidden_count // 2
    z = lax.axis_index("z")
    units = hidden_count // 256
    b_order = (
        b_in.reshape(2, 2, 2, 2, 2, 4, 2, units).transpose(4, 5, 3, 6, 2, 0, 1, 7).reshape(hidden_count)
    )
    b_mine = lax.dynamic_slice_in_dim(b_order, core * half, half)
    grad_flow = cotangent.astype(F4).reshape(pixels, channels)
    grad_mixed = grad_flow * layer_scale

    padded_low = between(tall, columns, 1)
    padded = padded_low.astype(F4)
    conv = jnp.zeros((row_count, col_count, channels), F4)
    for tap_row in range(7):
        for tap_col in range(7):
            conv = (
                conv
                + padded[tap_row : tap_row + row_count, tap_col : tap_col + col_count]
                * kernel[tap_row, tap_col]
            )
    average = jnp.mean(conv, -1, keepdims=True)
    centered = conv - average
    variance = jnp.mean(centered * centered, -1, keepdims=True)
    inv_std = lax.rsqrt(variance + 1e-06)
    unit_scaled = centered * inv_std
    normed = (unit_scaled * ln_gain + ln_bias).astype(BF).reshape(pixels, channels)
    ours = jnp.stack([normed, grad_mixed.astype(BF)], 0)
    theirs = swap(ours, "c", 1)
    normed_two = jnp.concatenate([ours[0], theirs[0]], 0)
    mixed_low = jnp.concatenate([ours[1], theirs[1]], 0)
    hidden = lax.dot_general(normed_two, w_in_t, contract_last, preferred_element_type=F4) + b_mine
    act_value, slope = gelu_parts(hidden)
    activated = act_value.astype(BF)
    grad_act = lax.dot_general(mixed_low, w_out_mine, contract_last, preferred_element_type=F4)
    grad_hidden = (grad_act * slope).astype(BF)
    grad_normed = jnp.dot(grad_hidden, w_in_t, preferred_element_type=F4)
    mixed = jnp.dot(activated, w_out_mine, preferred_element_type=F4)
    back = swap(jnp.stack([mixed[pixels:], grad_normed[pixels:]], 0).astype(BF), "c", 1)
    wout_term = lax.dot_general(activated, mixed_low, contract_first, preferred_element_type=F4)
    win_term = lax.dot_general(grad_hidden, normed_two, contract_first, preferred_element_type=F4)

    bias_mine = jnp.sum(grad_hidden.astype(F4), 0)
    bias_local = jnp.where(jnp.arange(2)[:, None] == core, bias_mine, 0.0)
    bias_local = (
        bias_local.reshape(2, 4, 2, 2, 2, 2, 2, units)
        .transpose(5, 6, 4, 2, 0, 1, 3, 7)
        .reshape(hidden_count // channels, channels)
    )
    index = jnp.stack(
        [core, lax.axis_index("x"), lax.axis_index(Y), z & 1, (z // 4) & 1, (z // 2) & 1]
    ).astype(jnp.int32)
    grad_low, mine, outer, block_out = local_call(
        norm_back,
        index,
        [
            shape(row_count, col_count, channels, dtype=BF),
            shape(SMALL + 3 * col_count, channels, dtype=BF),
            shape(3, col_count, channels, dtype=BF),
            shape(row_count, col_count, channels, dtype=BF),
        ],
        grad_normed, mixed, back, conv, ln_gain[None], padded_low, cotangent, feature_map,
        layer_scale[None], b_out[None], bias_local,
        scratch=[
            pltpu.VMEM((row_count, col_count, channels), F4),
            pltpu.VMEM((row_count + 6, col_count + 8, channels), F4),
            pltpu.VMEM((SMALL, channels), F4),
        ],
        flops=110 * pixels * channels,
    )
    theirs = swap(mine, "c", 1)
    outer_got = outer_swap(outer, ROW)
    rows = edge_order(theirs[SMALL:].reshape(3, col_count, channels), outer_got, ROW)
    low_tall = between(grad_low, rows, 0)

    small_shape = shape(SMALL, channels, dtype=BF)

    def message_of(rows, block=None):
        return shape(2 * (block or rows) + SMALL, channels, dtype=BF)

    def fan(messages, axis):
        return [swap(m, axis, flip) for m, flip in zip(messages, (1, 2, 3))]

    piece = half // 4
    *messages, shared = local_call(
        first_fan, index, [message_of(piece)] * 3 + [small_shape], win_term, wout_term, mine, theirs
    )
    got = fan(messages, "x")
    got, low_tall = lax.optimization_barrier((got, low_tall))
    total, *messages, shared = local_call(
        second_fan,
        index,
        [shape(2, piece, channels)] + [message_of(piece // 4)] * 3 + [small_shape],
        win_term, wout_term, shared, *got,
    )
    piece = piece // 4
    got = fan(messages, Y)
    columns = edges(low_tall, COL, 1)
    grad_pad = between(low_tall, columns, 1).astype(F4)
    total, message, shared = local_call(
        third_fan,
        index,
        [shape(2, piece, channels), message_of(up16(piece // 2)), small_shape],
        total, shared, *got,
    )
    for here, after, unit in ((3, 4, 1), (4, 5, 4)):
        piece = piece // 2
        got = swap(message, "z", unit)
        total, message, shared = local_call(
            functools.partial(pair_step, here, after),
            index,
            [shape(2, piece, channels), message_of(up16(piece // 2)), small_shape],
            total, shared, got,
        )
    got = swap(message, "z", 2)
    win_t, grad_w_out, small_grads, bias_rows = local_call(
        functools.partial(pair_end, 5),
        index,
        [shape(units, channels), shape(units, channels), shape(53, channels), shape(4, channels)],
        total, shared, got,
    )
    back_conv = jnp.zeros((row_count, col_count, channels), F4)
    for tap_row in range(7):
        for tap_col in range(7):
            back_conv = (
                back_conv
                + grad_pad[
                    6 - tap_row : 6 - tap_row + row_count, 6 - tap_col : 6 - tap_col + col_count
                ]
                * kernel[tap_row, tap_col]
            )
    grad_input = (cotangent.astype(F4) + back_conv).astype(BF)
    grad_b_in = bias_rows.reshape(hidden_count)
    return (block_out, grad_input, win_t.T, grad_w_out, small_grads, grad_b_in)


def solution(mesh):
    fine = Mesh(mesh.devices.reshape(8, 2, 2, 4, 2), ("z", "yh", "c", "x", "yl"))
    every = ROW + COL
    placed = (
        P(ROW, COL, None),
        P(),
        P(),
        P(),
        P(None, every),
        P(),
        P(every, None),
        P(),
        P(),
        P(ROW, COL, None),
    )
    return jax.shard_map(
        on_device,
        mesh=fine,
        in_specs=placed,
        out_specs=(
            P(ROW, COL, None),
            P(ROW, COL, None),
            P(None, every),
            P(every, None),
            P(),
            P(),
        ),
        check_vma=False,
    )
```

```python
import functools
import math

import jax
import jax.numpy as jnp
from jax import lax
from jax.experimental import pallas as pl
from jax.experimental.pallas import tpu as pltpu
from jax.sharding import Mesh
from jax.sharding import PartitionSpec as P

ROW = ("z", "yh", "c")
COL = ("x", "yl")
Y = ("yh", "yl")
BF = jnp.bfloat16
F4 = jnp.float32


def swap(x, axis, flip):
    count = lax.axis_size(axis)
    return lax.ppermute(x, axis, [(i, i ^ flip) for i in range(count)])


def edge_sends(x, axis, dim, width=3):
    length = x.shape[dim]
    odd = (lax.axis_index(axis) & 1) != 0
    last = lax.slice_in_dim(x, length - width, length, axis=dim)
    first = lax.slice_in_dim(x, 0, width, axis=dim)
    return jnp.where(odd, first, last), jnp.where(odd, last, first)


def outer_swap(x, axis):
    peers = lax.axis_size(axis)
    return lax.ppermute(x, axis, [(i, ((i + 1) ^ 1) - 1) for i in range(1, peers - 1)])


def edge_order(inner, outer, axis):
    odd = (lax.axis_index(axis) & 1) != 0
    return jnp.where(odd, inner, outer), jnp.where(odd, outer, inner)


def edges(x, axis, dim):
    inner, outer = edge_sends(x, axis, dim)
    return edge_order(swap(inner, axis, 1), outer_swap(outer, axis), axis)


def between(x, sides, dim):
    return jnp.concatenate([sides[0], x, sides[1]], axis=dim)


def gelu_parts(hidden):
    normal_cdf = 0.5 * (1.0 + jax.scipy.special.erf(hidden * (1.0 / math.sqrt(2.0))))
    density = jnp.exp(-0.5 * hidden * hidden) * (1.0 / math.sqrt(2.0 * math.pi))
    return (hidden * normal_cdf, normal_cdf + hidden * density)


def pair_gather(x, axis, bit):
    mine = (lax.axis_index(axis) & bit) != 0
    other = swap(x, axis, bit)
    return jnp.concatenate([jnp.where(mine, other, x), jnp.where(mine, x, other)], axis=1)


def quad_select(x, axis, unit):
    me = (lax.axis_index(axis) // unit) % 4
    parts = [x] + [swap(x, axis, flip * unit) for flip in (1, 2, 3)]
    low, high = (me & 1) != 0, (me & 2) != 0
    pairs = [(parts[0], parts[1]), (parts[2], parts[3])]
    ordered = [(jnp.where(low, q, p), jnp.where(low, p, q)) for p, q in pairs]
    first, second = ordered
    low_half = [jnp.where(high, q, p) for p, q in zip(first, second)]
    high_half = [jnp.where(high, p, q) for p, q in zip(first, second)]
    return jnp.concatenate(low_half + high_half, axis=1)


def quad_gather(x, axis, extra=None):
    me = lax.axis_index(axis)
    rows, channels = x.shape[1:]
    others = []
    for flip in (1, 2, 3):
        if flip == 1 and extra is not None:
            got = swap(jnp.concatenate([x.reshape(2 * rows, channels), extra], 0), axis, flip)
            others.append(got[: 2 * rows].reshape(x.shape))
            extra = got[2 * rows :]
        else:
            others.append(swap(x, axis, flip))
    full = jnp.zeros((x.shape[0], 4 * rows, channels), x.dtype)
    for flip, piece in zip((0, 1, 2, 3), [x] + others):
        full = lax.dynamic_update_slice_in_dim(full, piece, (me ^ flip) * rows, axis=1)
    return full if extra is None else (full, extra)


def local_call(kernel, index, outs, *arrays, scratch=(), flops=1_000_000):
    moved = sum(math.prod(a.shape) * a.dtype.itemsize for a in list(arrays) + list(outs))
    return pl.pallas_call(
        kernel,
        out_shape=outs,
        in_specs=[pl.BlockSpec(memory_space=pltpu.SMEM)]
        + [pl.BlockSpec(memory_space=pltpu.VMEM)] * len(arrays),
        out_specs=[pl.BlockSpec(memory_space=pltpu.VMEM)] * len(outs),
        scratch_shapes=list(scratch),
        cost_estimate=pl.CostEstimate(flops=flops, bytes_accessed=moved, transcendentals=0),
        compiler_params=pltpu.CompilerParams(vmem_limit_bytes=8 * 2**20),
    )(index, *arrays)


def shape(*dims, dtype=F4):
    return jax.ShapeDtypeStruct(dims, dtype)


SMALL = 64


def put_two(ref, at, value):
    high = value.astype(BF)
    ref[at : at + SMALL, :] = high
    ref[at + SMALL : at + 2 * SMALL, :] = (value - high.astype(F4)).astype(BF)


def get_two(ref, at):
    return ref[at : at + SMALL, :].astype(F4) + ref[at + SMALL : at + 2 * SMALL, :].astype(F4)


def norm_back(
    index, normed_grad, mixed, back, conv, gain, padded, cot, feature, scale, b_out, bias,
    low, message, outer, block_out, grads, wide, sums,
):
    rows, cols, channels = low.shape
    pixels = rows * cols

    def flat(x):
        return x.reshape(pixels, channels)

    taken = flat(conv[...])
    centered = taken - jnp.mean(taken, -1, keepdims=True)
    inv_std = lax.rsqrt(jnp.mean(centered * centered, -1, keepdims=True) + 1e-06)
    unit = centered * inv_std
    grad = normed_grad[0:pixels, :] + back[1].astype(F4)
    scaled = grad * gain[...]
    grad_conv = inv_std * (
        scaled
        - jnp.mean(scaled, -1, keepdims=True)
        - unit * jnp.mean(scaled * unit, -1, keepdims=True)
    )
    grads[...] = grad_conv.reshape(rows, cols, channels)
    low[...] = grad_conv.reshape(rows, cols, channels).astype(BF)
    sums[...] = jnp.zeros_like(sums)
    sums[49:50, :] = jnp.sum(grad * unit, 0, keepdims=True)
    sums[50:51, :] = jnp.sum(grad, 0, keepdims=True)
    full = mixed[0:pixels, :] + back[0].astype(F4) + b_out[...]
    flow = flat(cot[...].astype(F4))
    sums[51:52, :] = jnp.sum(flow * scale[...], 0, keepdims=True)
    sums[52:53, :] = jnp.sum(flow * full, 0, keepdims=True)
    sums[53:57, :] = bias[...]
    block_out[...] = (
        (flat(feature[...].astype(F4)) + scale[...] * full).astype(BF).reshape(rows, cols, channels)
    )
    for r in range(rows + 6):
        wide[r, 0 : cols + 6, :] = padded[r].astype(F4)
    for j in range(7):
        total = [jnp.zeros((8, channels), F4) for _ in range(7)]
        for r in range(rows + 6):
            slab = wide[r, j : j + cols, :]
            for p in range(max(0, r - 6), min(rows, r + 1)):
                term = slab * grads[p]
                term = tree([term[8 * k : 8 * k + 8] for k in range(cols // 8)])
                total[r - p] = total[r - p] + term
        for i in range(7):
            sums[7 * i + j : 7 * i + j + 1, :] = jnp.sum(total[i], 0, keepdims=True)
    put_two(message, 0, sums[...])
    odd = index[0] != 0
    first, last = grads[0:3], grads[rows - 3 : rows]
    message[2 * SMALL : 2 * SMALL + 3 * cols, :] = (
        jnp.where(odd, first, last).astype(BF).reshape(3 * cols, channels)
    )
    outer[...] = jnp.where(odd, last, first).astype(BF)


def first_fan(index, win, wout, mine, theirs, one, two, three, shared):
    rows = win.shape[0] // 4
    shared[...] = (get_two(mine, 0) + get_two(theirs, 0)).astype(BF)
    for flip, message in ((1, one), (2, two), (3, three)):
        at = pl.multiple_of((index[1] ^ flip) * rows, rows)
        message[0:rows, :] = win[pl.ds(at, rows), :].astype(BF)
        message[rows : 2 * rows, :] = wout[pl.ds(at, rows), :].astype(BF)
        message[2 * rows :, :] = shared[...]


def second_fan(index, win, wout, mine, g1, g2, g3, total, one, two, three, shared):
    rows = win.shape[0] // 4
    at = pl.multiple_of(index[1] * rows, rows)
    for k, term in enumerate((win, wout)):
        own = term[pl.ds(at, rows), :]
        got = [g[k * rows : (k + 1) * rows, :].astype(F4) for g in (g1, g2, g3)]
        total[k] = tree([own] + got)
    small = tree([mine[...].astype(F4)] + [g[2 * rows :, :].astype(F4) for g in (g1, g2, g3)])
    shared[...] = small.astype(BF)
    part = rows // 4
    for flip, message in ((1, one), (2, two), (3, three)):
        at = pl.multiple_of((index[2] ^ flip) * part, part)
        for k in range(2):
            message[k * part : (k + 1) * part, :] = total[k, pl.ds(at, part), :].astype(BF)
        message[2 * part :, :] = shared[...]


def up16(n):
    return -(-n // 16) * 16


def send_half(total, k, bit, message):
    half = total.shape[1] // 2
    block = up16(half)
    value = jnp.where(bit, total[k, 0:half, :], total[k, half : 2 * half, :])
    message[k * block : k * block + half, :] = value.astype(BF)


def third_fan(index, before, mine, g1, g2, g3, total, message, shared):
    rows = before.shape[1] // 4
    at = pl.multiple_of(index[2] * rows, rows)
    for k in range(2):
        got = [g[k * rows : (k + 1) * rows, :].astype(F4) for g in (g1, g2, g3)]
        total[k] = tree([before[k, pl.ds(at, rows), :]] + got)
    small = tree([mine[...].astype(F4)] + [g[2 * rows :, :].astype(F4) for g in (g1, g2, g3)])
    put_two(shared, 0, small)
    held = message.shape[0] - 2 * SMALL
    for k in range(2):
        send_half(total, k, index[3] != 0, message)
    message[held:, :] = shared[...]


def quarter(ref, k, which):
    rows = ref.shape[1] // 4
    parts = [ref[k, i * rows : (i + 1) * rows, :] for i in range(4)]
    low = [jnp.where((which & 1) != 0, q, p) for p, q in (parts[:2], parts[2:])]
    return jnp.where((which & 2) != 0, low[1], low[0])


def fourth_fan(index, before, mine, got, total, one, two, three, shared):
    half = before.shape[1] // 2
    block = up16(half)
    bit = index[3] != 0
    for k in range(2):
        own = jnp.where(bit, before[k, half : 2 * half, :], before[k, 0:half, :])
        total[k] = own + got[k * block : k * block + half, :].astype(F4)
    shared[...] = (get_two(mine, 0) + get_two(got, 2 * block)).astype(BF)
    rows = half // 4
    block = up16(rows)
    for flip, message in ((1, one), (2, two), (3, three)):
        for k in range(2):
            message[k * block : k * block + rows, :] = quarter(total, k, index[4] ^ flip).astype(BF)
        message[2 * block :, :] = shared[...]


def last_sum(index, before, mine, g1, g2, g3, win, wout, small, bias):
    rows = before.shape[1] // 4
    block = up16(rows)
    for k, out in ((0, win), (1, wout)):
        got = [g[k * block : k * block + rows, :].astype(F4) for g in (g1, g2, g3)]
        out[...] = tree([quarter(before, k, index[4])] + got)
    total = tree([mine[...].astype(F4)] + [g[2 * block :, :].astype(F4) for g in (g1, g2, g3)])
    small[...] = total[0:53, :]
    wide = total.shape[1]
    for i in range(4):
        bias[i * wide : (i + 1) * wide] = total[53 + i]


def conv_back(index, tall, left, right, taps, cot, out, wide):
    rows, cols, channels = out.shape
    for r in range(rows + 6):
        wide[r, 8 : 8 + cols, :] = tall[r].astype(F4)
        wide[r, 5:8, :] = left[r].astype(F4)
        wide[r, 8 + cols : 11 + cols, :] = right[r].astype(F4)
    for lane in range(0, channels, 128):
        total = [cot[p, :, lane : lane + 128].astype(F4) for p in range(rows)]
        for j in range(7):
            weights = [taps[7 * i + j : 7 * i + j + 1, lane : lane + 128] for i in range(7)]
            for r in range(rows + 6):
                slab = wide[r, 11 - j : 11 - j + cols, lane : lane + 128]
                for p in range(max(0, r - 6), min(rows, r + 1)):
                    total[p] = total[p] + slab * weights[6 - (r - p)]
        for p in range(rows):
            out[p, :, lane : lane + 128] = total[p].astype(BF)


def tree(parts):
    while len(parts) > 1:
        parts = [p + q for p, q in zip(parts[::2], parts[1::2])]
    return parts[0]


def on_device(
    feature_map, kernel, ln_gain, ln_bias, w_in, b_in, w_out, b_out, layer_scale, cotangent
):
    row_count, col_count, channels = feature_map.shape
    pixels = row_count * col_count
    hidden_count = b_in.shape[0]
    contract_last = (((1,), (1,)), ((), ()))
    contract_first = (((0,), (0,)), ((), ()))

    weights = jnp.stack([w_in.T, w_out], 0)
    weights = quad_select(weights, "z", 2)
    weights = pair_gather(weights, "z", 1)
    rows = edges(feature_map, ROW, 0)
    weights, feature_map, cotangent, rows = lax.optimization_barrier(
        (weights, feature_map, cotangent, rows)
    )
    tall = between(feature_map, rows, 0)
    inner, outer = edge_sends(tall, COL, 1)
    outer_got = outer_swap(outer, COL)
    weights, inner_got = quad_gather(weights, Y, inner.reshape(-1, channels))
    columns = edge_order(inner_got.reshape(inner.shape), outer_got, COL)
    weights, tall, columns, cotangent, kernel, ln_gain, layer_scale, b_out = lax.optimization_barrier(
        (weights, tall, columns, cotangent, kernel, ln_gain, layer_scale, b_out)
    )
    weights = quad_gather(weights, "x")
    w_in_t, w_out_mine = weights[0], weights[1]
    core = lax.axis_index("c")
    half = hidden_count // 2
    z = lax.axis_index("z")
    units = hidden_count // 256
    b_order = (
        b_in.reshape(2, 2, 2, 2, 2, 4, 2, units).transpose(4, 5, 3, 6, 2, 0, 1, 7).reshape(hidden_count)
    )
    b_mine = lax.dynamic_slice_in_dim(b_order, core * half, half)
    grad_flow = cotangent.astype(F4).reshape(pixels, channels)
    grad_mixed = grad_flow * layer_scale

    taps = kernel.reshape(-1, channels)
    padded_low = between(tall, columns, 1)
    padded = padded_low.astype(F4)
    conv = jnp.zeros((row_count, col_count, channels), F4)
    for tap_row in range(7):
        for tap_col in range(7):
            conv = (
                conv
                + padded[tap_row : tap_row + row_count, tap_col : tap_col + col_count]
                * kernel[tap_row, tap_col]
            )
    average = jnp.mean(conv, -1, keepdims=True)
    centered = conv - average
    variance = jnp.mean(centered * centered, -1, keepdims=True)
    inv_std = lax.rsqrt(variance + 1e-06)
    unit_scaled = centered * inv_std
    normed = (unit_scaled * ln_gain + ln_bias).astype(BF).reshape(pixels, channels)
    ours = jnp.stack([normed, grad_mixed.astype(BF)], 0)
    theirs = swap(ours, "c", 1)
    normed_two = jnp.concatenate([ours[0], theirs[0]], 0)
    mixed_low = jnp.concatenate([ours[1], theirs[1]], 0)
    hidden = lax.dot_general(normed_two, w_in_t, contract_last, preferred_element_type=F4) + b_mine
    act_value, slope = gelu_parts(hidden)
    activated = act_value.astype(BF)
    grad_act = lax.dot_general(mixed_low, w_out_mine, contract_last, preferred_element_type=F4)
    grad_hidden = (grad_act * slope).astype(BF)
    grad_normed = jnp.dot(grad_hidden, w_in_t, preferred_element_type=F4)
    mixed = jnp.dot(activated, w_out_mine, preferred_element_type=F4)
    back = swap(jnp.stack([mixed[pixels:], grad_normed[pixels:]], 0).astype(BF), "c", 1)
    wout_term = lax.dot_general(activated, mixed_low, contract_first, preferred_element_type=F4)
    win_term = lax.dot_general(grad_hidden, normed_two, contract_first, preferred_element_type=F4)

    bias_mine = jnp.sum(grad_hidden.astype(F4), 0)
    bias_local = jnp.where(jnp.arange(2)[:, None] == core, bias_mine, 0.0)
    bias_local = (
        bias_local.reshape(2, 4, 2, 2, 2, 2, 2, units)
        .transpose(5, 6, 4, 2, 0, 1, 3, 7)
        .reshape(hidden_count // channels, channels)
    )
    index = jnp.stack(
        [core, lax.axis_index("x"), lax.axis_index(Y), z & 1, z // 2]
    ).astype(jnp.int32)
    grad_low, mine, outer, block_out = local_call(
        norm_back,
        index,
        [
            shape(row_count, col_count, channels, dtype=BF),
            shape(2 * SMALL + 3 * col_count, channels, dtype=BF),
            shape(3, col_count, channels, dtype=BF),
            shape(row_count, col_count, channels, dtype=BF),
        ],
        grad_normed, mixed, back, conv, ln_gain[None], padded_low, cotangent, feature_map,
        layer_scale[None], b_out[None], bias_local,
        scratch=[
            pltpu.VMEM((row_count, col_count, channels), F4),
            pltpu.VMEM((row_count + 6, col_count + 8, channels), F4),
            pltpu.VMEM((SMALL, channels), F4),
        ],
        flops=110 * pixels * channels,
    )
    theirs = swap(mine, "c", 1)
    small_shape = shape(SMALL, channels, dtype=BF)

    def message_of(rows, smalls=1):
        return shape(2 * rows + smalls * SMALL, channels, dtype=BF)

    def fan(messages, axis, unit=1):
        return [swap(m, axis, flip * unit) for m, flip in zip(messages, (1, 2, 3))]

    piece = half // 4
    *messages, shared = local_call(
        first_fan, index, [message_of(piece)] * 3 + [small_shape], win_term, wout_term, mine, theirs
    )
    got = fan(messages, "x")
    first_got, outer = lax.optimization_barrier((got[0], outer))
    got[0] = first_got
    outer_got = outer_swap(outer, ROW)
    rows = edge_order(theirs[2 * SMALL :].reshape(3, col_count, channels), outer_got, ROW)
    low_tall = between(grad_low, rows, 0)
    columns = edges(low_tall, COL, 1)
    total, *messages, shared = local_call(
        second_fan,
        index,
        [shape(2, piece, channels)] + [message_of(piece // 4)] * 3 + [small_shape],
        win_term, wout_term, shared, *got,
    )
    piece = piece // 4
    got = fan(messages, Y)
    total, message, shared = local_call(
        third_fan,
        index,
        [
            shape(2, piece, channels),
            message_of(up16(piece // 2), 2),
            shape(2 * SMALL, channels, dtype=BF),
        ],
        total, shared, *got,
    )
    piece = piece // 2
    got = swap(message, "z", 1)
    total, *messages, shared = local_call(
        fourth_fan,
        index,
        [shape(2, piece, channels)] + [message_of(up16(units))] * 3 + [small_shape],
        total, shared, got,
    )
    got = fan(messages, "z", 2)
    win_t, grad_w_out, small_grads, grad_b_in = local_call(
        last_sum,
        index,
        [shape(units, channels), shape(units, channels), shape(53, channels), shape(hidden_count)],
        total, shared, *got,
    )
    (grad_input,) = local_call(
        conv_back,
        index,
        [shape(row_count, col_count, channels, dtype=BF)],
        low_tall, *columns, taps, cotangent,
        scratch=[pltpu.VMEM((row_count + 6, col_count + 16, channels), F4)],
        flops=98 * pixels * channels,
    )
    return (block_out, grad_input, win_t.T, grad_w_out, small_grads, grad_b_in)


def solution(mesh):
    fine = Mesh(mesh.devices.reshape(8, 2, 2, 4, 2), ("z", "yh", "c", "x", "yl"))
    every = ROW + COL
    placed = (
        P(ROW, COL, None),
        P(),
        P(),
        P(),
        P(None, every),
        P(),
        P(every, None),
        P(),
        P(),
        P(ROW, COL, None),
    )
    return jax.shard_map(
        on_device,
        mesh=fine,
        in_specs=placed,
        out_specs=(
            P(ROW, COL, None),
            P(ROW, COL, None),
            P(None, every),
            P(every, None),
            P(),
            P(),
        ),
        check_vma=False,
    )
```

```python
import functools
import math

import jax
import jax.numpy as jnp
from jax import lax
from jax.experimental import pallas as pl
from jax.experimental.pallas import tpu as pltpu
from jax.sharding import Mesh
from jax.sharding import PartitionSpec as P

ROW = ("z", "yh", "c")
COL = ("x", "yl")
Y = ("yh", "yl")
BF = jnp.bfloat16
F4 = jnp.float32


def swap(x, axis, flip):
    count = lax.axis_size(axis)
    return lax.ppermute(x, axis, [(i, i ^ flip) for i in range(count)])


def edge_sends(x, axis, dim, width=3):
    length = x.shape[dim]
    odd = (lax.axis_index(axis) & 1) != 0
    last = lax.slice_in_dim(x, length - width, length, axis=dim)
    first = lax.slice_in_dim(x, 0, width, axis=dim)
    return jnp.where(odd, first, last), jnp.where(odd, last, first)


def outer_swap(x, axis):
    peers = lax.axis_size(axis)
    return lax.ppermute(x, axis, [(i, ((i + 1) ^ 1) - 1) for i in range(1, peers - 1)])


def edge_order(inner, outer, axis):
    odd = (lax.axis_index(axis) & 1) != 0
    return jnp.where(odd, inner, outer), jnp.where(odd, outer, inner)


def edges(x, axis, dim):
    inner, outer = edge_sends(x, axis, dim)
    return edge_order(swap(inner, axis, 1), outer_swap(outer, axis), axis)


def between(x, sides, dim):
    return jnp.concatenate([sides[0], x, sides[1]], axis=dim)


def gelu_parts(hidden):
    normal_cdf = 0.5 * (1.0 + jax.scipy.special.erf(hidden * (1.0 / math.sqrt(2.0))))
    density = jnp.exp(-0.5 * hidden * hidden) * (1.0 / math.sqrt(2.0 * math.pi))
    return (hidden * normal_cdf, normal_cdf + hidden * density)


def pair_gather(x, axis, bit):
    mine = (lax.axis_index(axis) & bit) != 0
    other = swap(x, axis, bit)
    return jnp.concatenate([jnp.where(mine, other, x), jnp.where(mine, x, other)], axis=1)


def quad_select(x, axis, unit):
    me = (lax.axis_index(axis) // unit) % 4
    parts = [x] + [swap(x, axis, flip * unit) for flip in (1, 2, 3)]
    low, high = (me & 1) != 0, (me & 2) != 0
    pairs = [(parts[0], parts[1]), (parts[2], parts[3])]
    ordered = [(jnp.where(low, q, p), jnp.where(low, p, q)) for p, q in pairs]
    first, second = ordered
    low_half = [jnp.where(high, q, p) for p, q in zip(first, second)]
    high_half = [jnp.where(high, p, q) for p, q in zip(first, second)]
    return jnp.concatenate(low_half + high_half, axis=1)


def quad_gather(x, axis, extra=None):
    me = lax.axis_index(axis)
    rows, channels = x.shape[1:]
    others = {}
    for flip in (1, 3, 2):
        if flip == 1 and extra is not None:
            got = swap(jnp.concatenate([x.reshape(2 * rows, channels), extra], 0), axis, flip)
            others[flip] = got[: 2 * rows].reshape(x.shape)
            extra = got[2 * rows :]
        else:
            others[flip] = swap(x, axis, flip)
    full = jnp.zeros((x.shape[0], 4 * rows, channels), x.dtype)
    for flip, piece in ((0, x), (1, others[1]), (3, others[3]), (2, others[2])):
        full = lax.dynamic_update_slice_in_dim(full, piece, (me ^ flip) * rows, axis=1)
    return full if extra is None else (full, extra)


def local_call(kernel, index, outs, *arrays, scratch=(), flops=1_000_000):
    moved = sum(math.prod(a.shape) * a.dtype.itemsize for a in list(arrays) + list(outs))
    return pl.pallas_call(
        kernel,
        out_shape=outs,
        in_specs=[pl.BlockSpec(memory_space=pltpu.SMEM)]
        + [pl.BlockSpec(memory_space=pltpu.VMEM)] * len(arrays),
        out_specs=[pl.BlockSpec(memory_space=pltpu.VMEM)] * len(outs),
        scratch_shapes=list(scratch),
        cost_estimate=pl.CostEstimate(flops=flops, bytes_accessed=moved, transcendentals=0),
        compiler_params=pltpu.CompilerParams(vmem_limit_bytes=8 * 2**20),
    )(index, *arrays)


def shape(*dims, dtype=F4):
    return jax.ShapeDtypeStruct(dims, dtype)


SMALL = 64


def put_two(ref, at, value):
    high = value.astype(BF)
    ref[at : at + SMALL, :] = high
    ref[at + SMALL : at + 2 * SMALL, :] = (value - high.astype(F4)).astype(BF)


def get_two(ref, at):
    return ref[at : at + SMALL, :].astype(F4) + ref[at + SMALL : at + 2 * SMALL, :].astype(F4)


def norm_back(
    index, normed_grad, mixed, back, conv, gain, padded, cot, feature, scale, b_out, bias,
    low, message, outer, block_out, grads, wide, sums,
):
    rows, cols, channels = low.shape
    pixels = rows * cols

    def flat(x):
        return x.reshape(pixels, channels)

    taken = flat(conv[...])
    centered = taken - jnp.mean(taken, -1, keepdims=True)
    inv_std = lax.rsqrt(jnp.mean(centered * centered, -1, keepdims=True) + 1e-06)
    unit = centered * inv_std
    grad = normed_grad[0:pixels, :] + back[1].astype(F4)
    scaled = grad * gain[...]
    grad_conv = inv_std * (
        scaled
        - jnp.mean(scaled, -1, keepdims=True)
        - unit * jnp.mean(scaled * unit, -1, keepdims=True)
    )
    grads[...] = grad_conv.reshape(rows, cols, channels)
    low[...] = grad_conv.reshape(rows, cols, channels).astype(BF)
    sums[...] = jnp.zeros_like(sums)
    sums[49:50, :] = jnp.sum(grad * unit, 0, keepdims=True)
    sums[50:51, :] = jnp.sum(grad, 0, keepdims=True)
    full = mixed[0:pixels, :] + back[0].astype(F4) + b_out[...]
    flow = flat(cot[...].astype(F4))
    sums[51:52, :] = jnp.sum(flow * scale[...], 0, keepdims=True)
    sums[52:53, :] = jnp.sum(flow * full, 0, keepdims=True)
    sums[53:57, :] = bias[...]
    block_out[...] = (
        (flat(feature[...].astype(F4)) + scale[...] * full).astype(BF).reshape(rows, cols, channels)
    )
    for r in range(rows + 6):
        wide[r, 0 : cols + 6, :] = padded[r].astype(F4)
    for j in range(7):
        total = [jnp.zeros((8, channels), F4) for _ in range(7)]
        for r in range(rows + 6):
            slab = wide[r, j : j + cols, :]
            for p in range(max(0, r - 6), min(rows, r + 1)):
                term = slab * grads[p]
                term = tree([term[8 * k : 8 * k + 8] for k in range(cols // 8)])
                total[r - p] = total[r - p] + term
        for i in range(7):
            sums[7 * i + j : 7 * i + j + 1, :] = jnp.sum(total[i], 0, keepdims=True)
    put_two(message, 0, sums[...])
    odd = index[0] != 0
    first, last = grads[0:3], grads[rows - 3 : rows]
    message[2 * SMALL : 2 * SMALL + 3 * cols, :] = (
        jnp.where(odd, first, last).astype(BF).reshape(3 * cols, channels)
    )
    outer[...] = jnp.where(odd, last, first).astype(BF)


def first_fan(index, win, wout, mine, theirs, one, three, two, shared):
    rows = win.shape[0] // 4
    shared[...] = (get_two(mine, 0) + get_two(theirs, 0)).astype(BF)
    for flip, message in ((1, one), (3, three), (2, two)):
        at = pl.multiple_of((index[1] ^ flip) * rows, rows)
        message[0:rows, :] = win[pl.ds(at, rows), :].astype(BF)
        message[rows : 2 * rows, :] = wout[pl.ds(at, rows), :].astype(BF)
        message[2 * rows :, :] = shared[...]


def second_fan(index, win, wout, mine, g1, g3, g2, total, one, three, two, shared):
    rows = win.shape[0] // 4
    at = pl.multiple_of(index[1] * rows, rows)
    for k, term in enumerate((win, wout)):
        own = term[pl.ds(at, rows), :]
        got = [g[k * rows : (k + 1) * rows, :].astype(F4) for g in (g1, g2, g3)]
        total[k] = tree([own] + got)
    small = tree([mine[...].astype(F4)] + [g[2 * rows :, :].astype(F4) for g in (g1, g2, g3)])
    shared[...] = small.astype(BF)
    part = rows // 4
    for flip, message in ((1, one), (3, three), (2, two)):
        at = pl.multiple_of((index[2] ^ flip) * part, part)
        for k in range(2):
            message[k * part : (k + 1) * part, :] = total[k, pl.ds(at, part), :].astype(BF)
        message[2 * part :, :] = shared[...]


def up16(n):
    return -(-n // 16) * 16


def send_half(total, k, bit, message):
    half = total.shape[1] // 2
    block = up16(half)
    value = jnp.where(bit, total[k, 0:half, :], total[k, half : 2 * half, :])
    message[k * block : k * block + half, :] = value.astype(BF)


def third_fan(index, before, mine, g1, g3, g2, total, message, shared):
    rows = before.shape[1] // 4
    at = pl.multiple_of(index[2] * rows, rows)
    for k in range(2):
        got = [g[k * rows : (k + 1) * rows, :].astype(F4) for g in (g1, g2, g3)]
        total[k] = tree([before[k, pl.ds(at, rows), :]] + got)
    small = tree([mine[...].astype(F4)] + [g[2 * rows :, :].astype(F4) for g in (g1, g2, g3)])
    put_two(shared, 0, small)
    held = message.shape[0] - 2 * SMALL
    for k in range(2):
        send_half(total, k, index[3] != 0, message)
    message[held:, :] = shared[...]


def quarter(ref, k, which):
    rows = ref.shape[1] // 4
    parts = [ref[k, i * rows : (i + 1) * rows, :] for i in range(4)]
    low = [jnp.where((which & 1) != 0, q, p) for p, q in (parts[:2], parts[2:])]
    return jnp.where((which & 2) != 0, low[1], low[0])


def fourth_fan(index, before, mine, got, total, one, three, two, shared):
    half = before.shape[1] // 2
    block = up16(half)
    bit = index[3] != 0
    for k in range(2):
        own = jnp.where(bit, before[k, half : 2 * half, :], before[k, 0:half, :])
        total[k] = own + got[k * block : k * block + half, :].astype(F4)
    shared[...] = (get_two(mine, 0) + get_two(got, 2 * block)).astype(BF)
    rows = half // 4
    block = up16(rows)
    for flip, message in ((1, one), (3, three), (2, two)):
        for k in range(2):
            message[k * block : k * block + rows, :] = quarter(total, k, index[4] ^ flip).astype(BF)
        message[2 * block :, :] = shared[...]


def last_sum(index, before, mine, g1, g3, g2, win, wout, small, bias):
    rows = before.shape[1] // 4
    block = up16(rows)
    for k, out in ((0, win), (1, wout)):
        got = [g[k * block : k * block + rows, :].astype(F4) for g in (g1, g2, g3)]
        out[...] = tree([quarter(before, k, index[4])] + got)
    total = tree([mine[...].astype(F4)] + [g[2 * block :, :].astype(F4) for g in (g1, g2, g3)])
    small[...] = total[0:53, :]
    wide = total.shape[1]
    for i in range(4):
        bias[i * wide : (i + 1) * wide] = total[53 + i]


def conv_back(index, tall, left, right, taps, cot, out, wide):
    rows, cols, channels = out.shape
    for r in range(rows + 6):
        wide[r, 8 : 8 + cols, :] = tall[r].astype(F4)
        wide[r, 5:8, :] = left[r].astype(F4)
        wide[r, 8 + cols : 11 + cols, :] = right[r].astype(F4)
    for lane in range(0, channels, 128):
        total = [cot[p, :, lane : lane + 128].astype(F4) for p in range(rows)]
        for j in range(7):
            weights = [taps[7 * i + j : 7 * i + j + 1, lane : lane + 128] for i in range(7)]
            for r in range(rows + 6):
                slab = wide[r, 11 - j : 11 - j + cols, lane : lane + 128]
                for p in range(max(0, r - 6), min(rows, r + 1)):
                    total[p] = total[p] + slab * weights[6 - (r - p)]
        for p in range(rows):
            out[p, :, lane : lane + 128] = total[p].astype(BF)


def tree(parts):
    while len(parts) > 1:
        parts = [p + q for p, q in zip(parts[::2], parts[1::2])]
    return parts[0]


def on_device(
    feature_map, kernel, ln_gain, ln_bias, w_in, b_in, w_out, b_out, layer_scale, cotangent
):
    row_count, col_count, channels = feature_map.shape
    pixels = row_count * col_count
    hidden_count = b_in.shape[0]
    contract_last = (((1,), (1,)), ((), ()))
    contract_first = (((0,), (0,)), ((), ()))

    weights = jnp.stack([w_in.T, w_out], 0)
    weights = quad_select(weights, "z", 2)
    weights = pair_gather(weights, "z", 1)
    rows = edges(feature_map, ROW, 0)
    weights, feature_map, cotangent, rows = lax.optimization_barrier(
        (weights, feature_map, cotangent, rows)
    )
    tall = between(feature_map, rows, 0)
    inner, outer = edge_sends(tall, COL, 1)
    outer_got = outer_swap(outer, COL)
    weights, inner_got = quad_gather(weights, Y, inner.reshape(-1, channels))
    columns = edge_order(inner_got.reshape(inner.shape), outer_got, COL)
    weights, tall, cotangent, kernel, ln_gain, layer_scale, b_out = lax.optimization_barrier(
        (weights, tall, cotangent, kernel, ln_gain, layer_scale, b_out)
    )
    weights = quad_gather(weights, "x")
    w_in_t, w_out_mine = weights[0], weights[1]
    core = lax.axis_index("c")
    half = hidden_count // 2
    z = lax.axis_index("z")
    units = hidden_count // 256
    b_order = (
        b_in.reshape(2, 2, 2, 2, 2, 4, 2, units).transpose(4, 5, 3, 6, 2, 0, 1, 7).reshape(hidden_count)
    )
    b_mine = lax.dynamic_slice_in_dim(b_order, core * half, half)
    grad_flow = cotangent.astype(F4).reshape(pixels, channels)
    grad_mixed = grad_flow * layer_scale

    taps = kernel.reshape(-1, channels)
    padded_low = between(tall, columns, 1)
    padded = padded_low.astype(F4)
    conv = jnp.zeros((row_count, col_count, channels), F4)
    for tap_row in range(7):
        for tap_col in range(7):
            conv = (
                conv
                + padded[tap_row : tap_row + row_count, tap_col : tap_col + col_count]
                * kernel[tap_row, tap_col]
            )
    average = jnp.mean(conv, -1, keepdims=True)
    centered = conv - average
    variance = jnp.mean(centered * centered, -1, keepdims=True)
    inv_std = lax.rsqrt(variance + 1e-06)
    unit_scaled = centered * inv_std
    normed = (unit_scaled * ln_gain + ln_bias).astype(BF).reshape(pixels, channels)
    ours = jnp.stack([normed, grad_mixed.astype(BF)], 0)
    theirs = swap(ours, "c", 1)
    normed_two = jnp.concatenate([ours[0], theirs[0]], 0)
    mixed_low = jnp.concatenate([ours[1], theirs[1]], 0)
    hidden = lax.dot_general(normed_two, w_in_t, contract_last, preferred_element_type=F4) + b_mine
    act_value, slope = gelu_parts(hidden)
    activated = act_value.astype(BF)
    grad_act = lax.dot_general(mixed_low, w_out_mine, contract_last, preferred_element_type=F4)
    grad_hidden = (grad_act * slope).astype(BF)
    grad_normed = jnp.dot(grad_hidden, w_in_t, preferred_element_type=F4)
    mixed = jnp.dot(activated, w_out_mine, preferred_element_type=F4)
    back = swap(jnp.stack([mixed[pixels:], grad_normed[pixels:]], 0).astype(BF), "c", 1)
    wout_term = lax.dot_general(activated, mixed_low, contract_first, preferred_element_type=F4)
    win_term = lax.dot_general(grad_hidden, normed_two, contract_first, preferred_element_type=F4)

    bias_mine = jnp.sum(grad_hidden.astype(F4), 0)
    bias_local = jnp.where(jnp.arange(2)[:, None] == core, bias_mine, 0.0)
    bias_local = (
        bias_local.reshape(2, 4, 2, 2, 2, 2, 2, units)
        .transpose(5, 6, 4, 2, 0, 1, 3, 7)
        .reshape(hidden_count // channels, channels)
    )
    index = jnp.stack(
        [core, lax.axis_index("x"), lax.axis_index(Y), z & 1, z // 2]
    ).astype(jnp.int32)
    grad_low, mine, outer, block_out = local_call(
        norm_back,
        index,
        [
            shape(row_count, col_count, channels, dtype=BF),
            shape(2 * SMALL + 3 * col_count, channels, dtype=BF),
            shape(3, col_count, channels, dtype=BF),
            shape(row_count, col_count, channels, dtype=BF),
        ],
        grad_normed, mixed, back, conv, ln_gain[None], padded_low, cotangent, feature_map,
        layer_scale[None], b_out[None], bias_local,
        scratch=[
            pltpu.VMEM((row_count, col_count, channels), F4),
            pltpu.VMEM((row_count + 6, col_count + 8, channels), F4),
            pltpu.VMEM((SMALL, channels), F4),
        ],
        flops=110 * pixels * channels,
    )
    theirs = swap(mine, "c", 1)
    small_shape = shape(SMALL, channels, dtype=BF)

    def message_of(rows, smalls=1):
        return shape(2 * rows + smalls * SMALL, channels, dtype=BF)

    def fan(messages, axis, unit=1):
        return [swap(m, axis, flip * unit) for m, flip in zip(messages, (1, 3, 2))]

    piece = half // 4
    *messages, shared = local_call(
        first_fan, index, [message_of(piece)] * 3 + [small_shape], win_term, wout_term, mine, theirs
    )
    messages[2], outer = lax.optimization_barrier((messages[2], outer))
    got = fan(messages, "x")
    outer_got = outer_swap(outer, ROW)
    rows = edge_order(theirs[2 * SMALL :].reshape(3, col_count, channels), outer_got, ROW)
    low_tall = between(grad_low, rows, 0)
    columns = edges(low_tall, COL, 1)
    total, *messages, shared = local_call(
        second_fan,
        index,
        [shape(2, piece, channels)] + [message_of(piece // 4)] * 3 + [small_shape],
        win_term, wout_term, shared, *got,
    )
    piece = piece // 4
    got = fan(messages, Y)
    total, message, shared = local_call(
        third_fan,
        index,
        [
            shape(2, piece, channels),
            message_of(up16(piece // 2), 2),
            shape(2 * SMALL, channels, dtype=BF),
        ],
        total, shared, *got,
    )
    piece = piece // 2
    got = swap(message, "z", 1)
    total, *messages, shared = local_call(
        fourth_fan,
        index,
        [shape(2, piece, channels)] + [message_of(up16(units))] * 3 + [small_shape],
        total, shared, got,
    )
    got = fan(messages, "z", 2)
    win_t, grad_w_out, small_grads, grad_b_in = local_call(
        last_sum,
        index,
        [shape(units, channels), shape(units, channels), shape(53, channels), shape(hidden_count)],
        total, shared, *got,
    )
    (grad_input,) = local_call(
        conv_back,
        index,
        [shape(row_count, col_count, channels, dtype=BF)],
        low_tall, *columns, taps, cotangent,
        scratch=[pltpu.VMEM((row_count + 6, col_count + 16, channels), F4)],
        flops=98 * pixels * channels,
    )
    return (block_out, grad_input, win_t.T, grad_w_out, small_grads, grad_b_in)


def solution(mesh):
    fine = Mesh(mesh.devices.reshape(8, 2, 2, 4, 2), ("z", "yh", "c", "x", "yl"))
    every = ROW + COL
    placed = (
        P(ROW, COL, None),
        P(),
        P(),
        P(),
        P(None, every),
        P(),
        P(every, None),
        P(),
        P(),
        P(ROW, COL, None),
    )
    return jax.shard_map(
        on_device,
        mesh=fine,
        in_specs=placed,
        out_specs=(
            P(ROW, COL, None),
            P(ROW, COL, None),
            P(None, every),
            P(every, None),
            P(),
            P(),
        ),
        check_vma=False,
    )
```

```python
import functools
import math

import jax
import jax.numpy as jnp
from jax import lax
from jax.experimental import pallas as pl
from jax.experimental.pallas import tpu as pltpu
from jax.sharding import Mesh
from jax.sharding import PartitionSpec as P

ROW = ("z", "yh", "c")
COL = ("x", "yl")
Y = ("yh", "yl")
BF = jnp.bfloat16
F4 = jnp.float32


def swap(x, axis, flip):
    count = lax.axis_size(axis)
    return lax.ppermute(x, axis, [(i, i ^ flip) for i in range(count)])


def edge_sends(x, axis, dim, width=3):
    length = x.shape[dim]
    odd = (lax.axis_index(axis) & 1) != 0
    last = lax.slice_in_dim(x, length - width, length, axis=dim)
    first = lax.slice_in_dim(x, 0, width, axis=dim)
    return jnp.where(odd, first, last), jnp.where(odd, last, first)


def outer_swap(x, axis):
    peers = lax.axis_size(axis)
    return lax.ppermute(x, axis, [(i, ((i + 1) ^ 1) - 1) for i in range(1, peers - 1)])


def edge_order(inner, outer, axis):
    odd = (lax.axis_index(axis) & 1) != 0
    return jnp.where(odd, inner, outer), jnp.where(odd, outer, inner)


def edges(x, axis, dim):
    inner, outer = edge_sends(x, axis, dim)
    return edge_order(swap(inner, axis, 1), outer_swap(outer, axis), axis)


def between(x, sides, dim):
    return jnp.concatenate([sides[0], x, sides[1]], axis=dim)


def gelu_parts(hidden):
    normal_cdf = 0.5 * (1.0 + jax.scipy.special.erf(hidden * (1.0 / math.sqrt(2.0))))
    density = jnp.exp(-0.5 * hidden * hidden) * (1.0 / math.sqrt(2.0 * math.pi))
    return (hidden * normal_cdf, normal_cdf + hidden * density)


def pair_gather(x, axis, bit):
    mine = (lax.axis_index(axis) & bit) != 0
    other = swap(x, axis, bit)
    return jnp.concatenate([jnp.where(mine, other, x), jnp.where(mine, x, other)], axis=1)


def quad_select(x, axis, unit):
    me = (lax.axis_index(axis) // unit) % 4
    parts = [x] + [swap(x, axis, flip * unit) for flip in (1, 2, 3)]
    low, high = (me & 1) != 0, (me & 2) != 0
    pairs = [(parts[0], parts[1]), (parts[2], parts[3])]
    ordered = [(jnp.where(low, q, p), jnp.where(low, p, q)) for p, q in pairs]
    first, second = ordered
    low_half = [jnp.where(high, q, p) for p, q in zip(first, second)]
    high_half = [jnp.where(high, p, q) for p, q in zip(first, second)]
    return jnp.concatenate(low_half + high_half, axis=1)


def quad_gather(x, axis, extra=None):
    me = lax.axis_index(axis)
    rows, channels = x.shape[1:]
    others = {}
    for flip in (1, 3, 2):
        if flip == 1 and extra is not None:
            got = swap(jnp.concatenate([x.reshape(2 * rows, channels), extra], 0), axis, flip)
            others[flip] = got[: 2 * rows].reshape(x.shape)
            extra = got[2 * rows :]
        else:
            others[flip] = swap(x, axis, flip)
    full = jnp.zeros((x.shape[0], 4 * rows, channels), x.dtype)
    order = (0, 1, 3, 2) if extra is None else (0, 2, 1, 3)
    for flip in order:
        piece = x if flip == 0 else others[flip]
        full = lax.dynamic_update_slice_in_dim(full, piece, (me ^ flip) * rows, axis=1)
    return full if extra is None else (full, extra)


def local_call(kernel, index, outs, *arrays, scratch=(), flops=1_000_000):
    moved = sum(math.prod(a.shape) * a.dtype.itemsize for a in list(arrays) + list(outs))
    return pl.pallas_call(
        kernel,
        out_shape=outs,
        in_specs=[pl.BlockSpec(memory_space=pltpu.SMEM)]
        + [pl.BlockSpec(memory_space=pltpu.VMEM)] * len(arrays),
        out_specs=[pl.BlockSpec(memory_space=pltpu.VMEM)] * len(outs),
        scratch_shapes=list(scratch),
        cost_estimate=pl.CostEstimate(flops=flops, bytes_accessed=moved, transcendentals=0),
        compiler_params=pltpu.CompilerParams(vmem_limit_bytes=8 * 2**20),
    )(index, *arrays)


def shape(*dims, dtype=F4):
    return jax.ShapeDtypeStruct(dims, dtype)


SMALL = 64


def put_two(ref, at, value):
    high = value.astype(BF)
    ref[at : at + SMALL, :] = high
    ref[at + SMALL : at + 2 * SMALL, :] = (value - high.astype(F4)).astype(BF)


def get_two(ref, at):
    return ref[at : at + SMALL, :].astype(F4) + ref[at + SMALL : at + 2 * SMALL, :].astype(F4)


def norm_back(
    index, normed_grad, mixed, back, conv, gain, padded, cot, feature, scale, b_out, bias,
    low, message, outer, block_out, grads, wide, sums,
):
    rows, cols, channels = low.shape
    pixels = rows * cols

    def flat(x):
        return x.reshape(pixels, channels)

    taken = flat(conv[...])
    centered = taken - jnp.mean(taken, -1, keepdims=True)
    inv_std = lax.rsqrt(jnp.mean(centered * centered, -1, keepdims=True) + 1e-06)
    unit = centered * inv_std
    grad = normed_grad[0:pixels, :] + back[1].astype(F4)
    scaled = grad * gain[...]
    grad_conv = inv_std * (
        scaled
        - jnp.mean(scaled, -1, keepdims=True)
        - unit * jnp.mean(scaled * unit, -1, keepdims=True)
    )
    grads[...] = grad_conv.reshape(rows, cols, channels)
    low[...] = grad_conv.reshape(rows, cols, channels).astype(BF)
    sums[...] = jnp.zeros_like(sums)
    sums[49:50, :] = jnp.sum(grad * unit, 0, keepdims=True)
    sums[50:51, :] = jnp.sum(grad, 0, keepdims=True)
    full = mixed[0:pixels, :] + back[0].astype(F4) + b_out[...]
    flow = flat(cot[...].astype(F4))
    sums[51:52, :] = jnp.sum(flow * scale[...], 0, keepdims=True)
    sums[52:53, :] = jnp.sum(flow * full, 0, keepdims=True)
    sums[53:57, :] = bias[...]
    block_out[...] = (
        (flat(feature[...].astype(F4)) + scale[...] * full).astype(BF).reshape(rows, cols, channels)
    )
    for r in range(rows + 6):
        wide[r, 0 : cols + 6, :] = padded[r].astype(F4)
    for j in range(7):
        total = [jnp.zeros((8, channels), F4) for _ in range(7)]
        for r in range(rows + 6):
            slab = wide[r, j : j + cols, :]
            for p in range(max(0, r - 6), min(rows, r + 1)):
                term = slab * grads[p]
                term = tree([term[8 * k : 8 * k + 8] for k in range(cols // 8)])
                total[r - p] = total[r - p] + term
        for i in range(7):
            sums[7 * i + j : 7 * i + j + 1, :] = jnp.sum(total[i], 0, keepdims=True)
    put_two(message, 0, sums[...])
    odd = index[0] != 0
    first, last = grads[0:3], grads[rows - 3 : rows]
    message[2 * SMALL : 2 * SMALL + 3 * cols, :] = (
        jnp.where(odd, first, last).astype(BF).reshape(3 * cols, channels)
    )
    outer[...] = jnp.where(odd, last, first).astype(BF)


def first_fan(index, win, wout, mine, theirs, one, three, two, shared):
    rows = win.shape[0] // 4
    shared[...] = (get_two(mine, 0) + get_two(theirs, 0)).astype(BF)
    for flip, message in ((1, one), (3, three), (2, two)):
        at = pl.multiple_of((index[1] ^ flip) * rows, rows)
        message[0:rows, :] = win[pl.ds(at, rows), :].astype(BF)
        message[rows : 2 * rows, :] = wout[pl.ds(at, rows), :].astype(BF)
        message[2 * rows :, :] = shared[...]


def second_fan(index, win, wout, mine, g1, g3, g2, total, two, one, three, shared):
    rows = win.shape[0] // 4
    at = pl.multiple_of(index[1] * rows, rows)
    for k, term in enumerate((win, wout)):
        own = term[pl.ds(at, rows), :]
        got = [g[k * rows : (k + 1) * rows, :].astype(F4) for g in (g1, g2, g3)]
        total[k] = tree([own] + got)
    small = tree([mine[...].astype(F4)] + [g[2 * rows :, :].astype(F4) for g in (g1, g2, g3)])
    shared[...] = small.astype(BF)
    part = rows // 4
    for flip, message in ((1, one), (3, three), (2, two)):
        at = pl.multiple_of((index[2] ^ flip) * part, part)
        for k in range(2):
            message[k * part : (k + 1) * part, :] = total[k, pl.ds(at, part), :].astype(BF)
        message[2 * part :, :] = shared[...]


def up16(n):
    return -(-n // 16) * 16


def send_half(total, k, bit, message):
    half = total.shape[1] // 2
    block = up16(half)
    value = jnp.where(bit, total[k, 0:half, :], total[k, half : 2 * half, :])
    message[k * block : k * block + half, :] = value.astype(BF)


def third_fan(index, before, mine, g2, g1, g3, total, message, shared):
    rows = before.shape[1] // 4
    at = pl.multiple_of(index[2] * rows, rows)
    for k in range(2):
        got = [g[k * rows : (k + 1) * rows, :].astype(F4) for g in (g1, g2, g3)]
        total[k] = tree([before[k, pl.ds(at, rows), :]] + got)
    small = tree([mine[...].astype(F4)] + [g[2 * rows :, :].astype(F4) for g in (g1, g2, g3)])
    put_two(shared, 0, small)
    held = message.shape[0] - 2 * SMALL
    for k in range(2):
        send_half(total, k, index[3] != 0, message)
    message[held:, :] = shared[...]


def quarter(ref, k, which):
    rows = ref.shape[1] // 4
    parts = [ref[k, i * rows : (i + 1) * rows, :] for i in range(4)]
    low = [jnp.where((which & 1) != 0, q, p) for p, q in (parts[:2], parts[2:])]
    return jnp.where((which & 2) != 0, low[1], low[0])


def fourth_fan(index, before, mine, got, total, two, one, three, shared):
    half = before.shape[1] // 2
    block = up16(half)
    bit = index[3] != 0
    for k in range(2):
        own = jnp.where(bit, before[k, half : 2 * half, :], before[k, 0:half, :])
        total[k] = own + got[k * block : k * block + half, :].astype(F4)
    shared[...] = (get_two(mine, 0) + get_two(got, 2 * block)).astype(BF)
    rows = half // 4
    block = up16(rows)
    for flip, message in ((1, one), (3, three), (2, two)):
        for k in range(2):
            message[k * block : k * block + rows, :] = quarter(total, k, index[4] ^ flip).astype(BF)
        message[2 * block :, :] = shared[...]


def last_sum(index, before, mine, g2, g1, g3, win, wout, small, bias):
    rows = before.shape[1] // 4
    block = up16(rows)
    for k, out in ((0, win), (1, wout)):
        got = [g[k * block : k * block + rows, :].astype(F4) for g in (g1, g2, g3)]
        out[...] = tree([quarter(before, k, index[4])] + got)
    total = tree([mine[...].astype(F4)] + [g[2 * block :, :].astype(F4) for g in (g1, g2, g3)])
    small[...] = total[0:53, :]
    wide = total.shape[1]
    for i in range(4):
        bias[i * wide : (i + 1) * wide] = total[53 + i]


def conv_back(index, tall, left, right, taps, cot, out, wide):
    rows, cols, channels = out.shape
    for r in range(rows + 6):
        wide[r, 8 : 8 + cols, :] = tall[r].astype(F4)
        wide[r, 5:8, :] = left[r].astype(F4)
        wide[r, 8 + cols : 11 + cols, :] = right[r].astype(F4)
    for lane in range(0, channels, 128):
        total = [cot[p, :, lane : lane + 128].astype(F4) for p in range(rows)]
        for j in range(7):
            weights = [taps[7 * i + j : 7 * i + j + 1, lane : lane + 128] for i in range(7)]
            for r in range(rows + 6):
                slab = wide[r, 11 - j : 11 - j + cols, lane : lane + 128]
                for p in range(max(0, r - 6), min(rows, r + 1)):
                    total[p] = total[p] + slab * weights[6 - (r - p)]
        for p in range(rows):
            out[p, :, lane : lane + 128] = total[p].astype(BF)


def tree(parts):
    while len(parts) > 1:
        parts = [p + q for p, q in zip(parts[::2], parts[1::2])]
    return parts[0]


def on_device(
    feature_map, kernel, ln_gain, ln_bias, w_in, b_in, w_out, b_out, layer_scale, cotangent
):
    row_count, col_count, channels = feature_map.shape
    pixels = row_count * col_count
    hidden_count = b_in.shape[0]
    contract_last = (((1,), (1,)), ((), ()))
    contract_first = (((0,), (0,)), ((), ()))

    weights = jnp.stack([w_in.T, w_out], 0)
    weights = quad_select(weights, "z", 2)
    weights = pair_gather(weights, "z", 1)
    rows = edges(feature_map, ROW, 0)
    weights, feature_map, cotangent, rows = lax.optimization_barrier(
        (weights, feature_map, cotangent, rows)
    )
    tall = between(feature_map, rows, 0)
    inner, outer = edge_sends(tall, COL, 1)
    outer_got = outer_swap(outer, COL)
    weights, inner_got = quad_gather(weights, Y, inner.reshape(-1, channels))
    columns = edge_order(inner_got.reshape(inner.shape), outer_got, COL)
    weights, tall, cotangent, kernel, ln_gain, layer_scale, b_out = lax.optimization_barrier(
        (weights, tall, cotangent, kernel, ln_gain, layer_scale, b_out)
    )
    weights = quad_gather(weights, "x")
    w_in_t, w_out_mine = weights[0], weights[1]
    core = lax.axis_index("c")
    half = hidden_count // 2
    z = lax.axis_index("z")
    units = hidden_count // 256
    b_order = (
        b_in.reshape(2, 2, 2, 2, 2, 4, 2, units).transpose(4, 5, 3, 6, 2, 0, 1, 7).reshape(hidden_count)
    )
    b_mine = lax.dynamic_slice_in_dim(b_order, core * half, half)
    grad_flow = cotangent.astype(F4).reshape(pixels, channels)
    grad_mixed = grad_flow * layer_scale

    taps = kernel.reshape(-1, channels)
    padded_low = between(tall, columns, 1)
    padded = padded_low.astype(F4)
    conv = jnp.zeros((row_count, col_count, channels), F4)
    for tap_row in range(7):
        for tap_col in range(7):
            conv = (
                conv
                + padded[tap_row : tap_row + row_count, tap_col : tap_col + col_count]
                * kernel[tap_row, tap_col]
            )
    average = jnp.mean(conv, -1, keepdims=True)
    centered = conv - average
    variance = jnp.mean(centered * centered, -1, keepdims=True)
    inv_std = lax.rsqrt(variance + 1e-06)
    unit_scaled = centered * inv_std
    normed = (unit_scaled * ln_gain + ln_bias).astype(BF).reshape(pixels, channels)
    ours = jnp.stack([normed, grad_mixed.astype(BF)], 0)
    theirs = swap(ours, "c", 1)
    normed_two = jnp.concatenate([ours[0], theirs[0]], 0)
    mixed_low = jnp.concatenate([ours[1], theirs[1]], 0)
    hidden = lax.dot_general(normed_two, w_in_t, contract_last, preferred_element_type=F4) + b_mine
    act_value, slope = gelu_parts(hidden)
    activated = act_value.astype(BF)
    grad_act = lax.dot_general(mixed_low, w_out_mine, contract_last, preferred_element_type=F4)
    grad_hidden = (grad_act * slope).astype(BF)
    grad_normed = jnp.dot(grad_hidden, w_in_t, preferred_element_type=F4)
    mixed = jnp.dot(activated, w_out_mine, preferred_element_type=F4)
    back = swap(jnp.stack([mixed[pixels:], grad_normed[pixels:]], 0).astype(BF), "c", 1)
    wout_term = lax.dot_general(activated, mixed_low, contract_first, preferred_element_type=F4)
    win_term = lax.dot_general(grad_hidden, normed_two, contract_first, preferred_element_type=F4)

    bias_mine = jnp.sum(grad_hidden.astype(F4), 0)
    bias_local = jnp.where(jnp.arange(2)[:, None] == core, bias_mine, 0.0)
    bias_local = (
        bias_local.reshape(2, 4, 2, 2, 2, 2, 2, units)
        .transpose(5, 6, 4, 2, 0, 1, 3, 7)
        .reshape(hidden_count // channels, channels)
    )
    index = jnp.stack(
        [core, lax.axis_index("x"), lax.axis_index(Y), z & 1, z // 2]
    ).astype(jnp.int32)
    grad_low, mine, outer, block_out = local_call(
        norm_back,
        index,
        [
            shape(row_count, col_count, channels, dtype=BF),
            shape(2 * SMALL + 3 * col_count, channels, dtype=BF),
            shape(3, col_count, channels, dtype=BF),
            shape(row_count, col_count, channels, dtype=BF),
        ],
        grad_normed, mixed, back, conv, ln_gain[None], padded_low, cotangent, feature_map,
        layer_scale[None], b_out[None], bias_local,
        scratch=[
            pltpu.VMEM((row_count, col_count, channels), F4),
            pltpu.VMEM((row_count + 6, col_count + 8, channels), F4),
            pltpu.VMEM((SMALL, channels), F4),
        ],
        flops=110 * pixels * channels,
    )
    theirs = swap(mine, "c", 1)
    small_shape = shape(SMALL, channels, dtype=BF)

    def message_of(rows, smalls=1):
        return shape(2 * rows + smalls * SMALL, channels, dtype=BF)

    def fan(messages, axis, flips, unit=1):
        return [swap(m, axis, flip * unit) for m, flip in zip(messages, flips)]

    piece = half // 4
    *messages, shared = local_call(
        first_fan, index, [message_of(piece)] * 3 + [small_shape], win_term, wout_term, mine, theirs
    )
    messages[2], outer = lax.optimization_barrier((messages[2], outer))
    got = fan(messages, "x", (1, 3, 2))
    outer_got = outer_swap(outer, ROW)
    rows = edge_order(theirs[2 * SMALL :].reshape(3, col_count, channels), outer_got, ROW)
    low_tall = between(grad_low, rows, 0)
    columns = edges(low_tall, COL, 1)
    total, *messages, shared = local_call(
        second_fan,
        index,
        [shape(2, piece, channels)] + [message_of(piece // 4)] * 3 + [small_shape],
        win_term, wout_term, shared, *got,
    )
    piece = piece // 4
    got = fan(messages, Y, (2, 1, 3))
    total, message, shared = local_call(
        third_fan,
        index,
        [
            shape(2, piece, channels),
            message_of(up16(piece // 2), 2),
            shape(2 * SMALL, channels, dtype=BF),
        ],
        total, shared, *got,
    )
    piece = piece // 2
    got = swap(message, "z", 1)
    total, *messages, shared = local_call(
        fourth_fan,
        index,
        [shape(2, piece, channels)] + [message_of(up16(units))] * 3 + [small_shape],
        total, shared, got,
    )
    got = fan(messages, "z", (2, 1, 3), 2)
    win_t, grad_w_out, small_grads, grad_b_in = local_call(
        last_sum,
        index,
        [shape(units, channels), shape(units, channels), shape(53, channels), shape(hidden_count)],
        total, shared, *got,
    )
    (grad_input,) = local_call(
        conv_back,
        index,
        [shape(row_count, col_count, channels, dtype=BF)],
        low_tall, *columns, taps, cotangent,
        scratch=[pltpu.VMEM((row_count + 6, col_count + 16, channels), F4)],
        flops=98 * pixels * channels,
    )
    return (block_out, grad_input, win_t.T, grad_w_out, small_grads, grad_b_in)


def solution(mesh):
    fine = Mesh(mesh.devices.reshape(8, 2, 2, 4, 2), ("z", "yh", "c", "x", "yl"))
    every = ROW + COL
    placed = (
        P(ROW, COL, None),
        P(),
        P(),
        P(),
        P(None, every),
        P(),
        P(every, None),
        P(),
        P(),
        P(ROW, COL, None),
    )
    return jax.shard_map(
        on_device,
        mesh=fine,
        in_specs=placed,
        out_specs=(
            P(ROW, COL, None),
            P(ROW, COL, None),
            P(None, every),
            P(every, None),
            P(),
            P(),
        ),
        check_vma=False,
    )
```

```python
import functools
import math

import jax
import jax.numpy as jnp
from jax import lax
from jax.experimental import pallas as pl
from jax.experimental.pallas import tpu as pltpu
from jax.sharding import Mesh
from jax.sharding import PartitionSpec as P

ROW = ("z", "yh", "c")
COL = ("x", "yl")
Y = ("yh", "yl")
BF = jnp.bfloat16
F4 = jnp.float32


def swap(x, axis, flip):
    count = lax.axis_size(axis)
    return lax.ppermute(x, axis, [(i, i ^ flip) for i in range(count)])


def edge_sends(x, axis, dim, width=3):
    length = x.shape[dim]
    odd = (lax.axis_index(axis) & 1) != 0
    last = lax.slice_in_dim(x, length - width, length, axis=dim)
    first = lax.slice_in_dim(x, 0, width, axis=dim)
    return jnp.where(odd, first, last), jnp.where(odd, last, first)


def outer_swap(x, axis):
    peers = lax.axis_size(axis)
    return lax.ppermute(x, axis, [(i, ((i + 1) ^ 1) - 1) for i in range(1, peers - 1)])


def edge_order(inner, outer, axis):
    odd = (lax.axis_index(axis) & 1) != 0
    return jnp.where(odd, inner, outer), jnp.where(odd, outer, inner)


def edges(x, axis, dim):
    inner, outer = edge_sends(x, axis, dim)
    return edge_order(swap(inner, axis, 1), outer_swap(outer, axis), axis)


def between(x, sides, dim):
    return jnp.concatenate([sides[0], x, sides[1]], axis=dim)


def gelu_parts(hidden):
    normal_cdf = 0.5 * (1.0 + jax.scipy.special.erf(hidden * (1.0 / math.sqrt(2.0))))
    density = jnp.exp(-0.5 * hidden * hidden) * (1.0 / math.sqrt(2.0 * math.pi))
    return (hidden * normal_cdf, normal_cdf + hidden * density)


def pair_gather(x, axis, bit):
    mine = (lax.axis_index(axis) & bit) != 0
    other = swap(x, axis, bit)
    return jnp.concatenate([jnp.where(mine, other, x), jnp.where(mine, x, other)], axis=1)


def quad_select(x, axis, unit):
    me = (lax.axis_index(axis) // unit) % 4
    parts = [x] + [swap(x, axis, flip * unit) for flip in (1, 2, 3)]
    low, high = (me & 1) != 0, (me & 2) != 0
    pairs = [(parts[0], parts[1]), (parts[2], parts[3])]
    ordered = [(jnp.where(low, q, p), jnp.where(low, p, q)) for p, q in pairs]
    first, second = ordered
    low_half = [jnp.where(high, q, p) for p, q in zip(first, second)]
    high_half = [jnp.where(high, p, q) for p, q in zip(first, second)]
    return jnp.concatenate(low_half + high_half, axis=1)


def quad_gather(x, axis, extra=None):
    me = lax.axis_index(axis)
    rows, channels = x.shape[1:]
    others = {}
    for flip in (1, 3, 2):
        if flip == 1 and extra is not None:
            got = swap(jnp.concatenate([x.reshape(2 * rows, channels), extra], 0), axis, flip)
            others[flip] = got[: 2 * rows].reshape(x.shape)
            extra = got[2 * rows :]
        else:
            others[flip] = swap(x, axis, flip)
    full = jnp.zeros((x.shape[0], 4 * rows, channels), x.dtype)
    order = (0, 1, 3, 2) if extra is None else (0, 2, 1, 3)
    for flip in order:
        piece = x if flip == 0 else others[flip]
        full = lax.dynamic_update_slice_in_dim(full, piece, (me ^ flip) * rows, axis=1)
    return full if extra is None else (full, extra)


def local_call(kernel, index, outs, *arrays, scratch=(), flops=1_000_000):
    moved = sum(math.prod(a.shape) * a.dtype.itemsize for a in list(arrays) + list(outs))
    return pl.pallas_call(
        kernel,
        out_shape=outs,
        in_specs=[pl.BlockSpec(memory_space=pltpu.SMEM)]
        + [pl.BlockSpec(memory_space=pltpu.VMEM)] * len(arrays),
        out_specs=[pl.BlockSpec(memory_space=pltpu.VMEM)] * len(outs),
        scratch_shapes=list(scratch),
        cost_estimate=pl.CostEstimate(flops=flops, bytes_accessed=moved, transcendentals=0),
        compiler_params=pltpu.CompilerParams(vmem_limit_bytes=8 * 2**20),
    )(index, *arrays)


def shape(*dims, dtype=F4):
    return jax.ShapeDtypeStruct(dims, dtype)


SMALL = 64


def put_two(ref, at, value):
    high = value.astype(BF)
    ref[at : at + SMALL, :] = high
    ref[at + SMALL : at + 2 * SMALL, :] = (value - high.astype(F4)).astype(BF)


def get_two(ref, at):
    return ref[at : at + SMALL, :].astype(F4) + ref[at + SMALL : at + 2 * SMALL, :].astype(F4)


def norm_back(
    index, normed_grad, mixed, back, conv, gain, padded, cot, feature, scale, b_out, bias,
    low, message, outer, block_out, grads, wide, sums,
):
    rows, cols, channels = low.shape
    pixels = rows * cols

    def flat(x):
        return x.reshape(pixels, channels)

    taken = flat(conv[...])
    centered = taken - jnp.mean(taken, -1, keepdims=True)
    inv_std = lax.rsqrt(jnp.mean(centered * centered, -1, keepdims=True) + 1e-06)
    unit = centered * inv_std
    grad = normed_grad[0:pixels, :] + back[1].astype(F4)
    scaled = grad * gain[...]
    grad_conv = inv_std * (
        scaled
        - jnp.mean(scaled, -1, keepdims=True)
        - unit * jnp.mean(scaled * unit, -1, keepdims=True)
    )
    grads[...] = grad_conv.reshape(rows, cols, channels)
    low[...] = grad_conv.reshape(rows, cols, channels).astype(BF)
    sums[...] = jnp.zeros_like(sums)
    sums[49:50, :] = jnp.sum(grad * unit, 0, keepdims=True)
    sums[50:51, :] = jnp.sum(grad, 0, keepdims=True)
    full = mixed[0:pixels, :] + back[0].astype(F4) + b_out[...]
    flow = flat(cot[...].astype(F4))
    sums[51:52, :] = jnp.sum(flow * scale[...], 0, keepdims=True)
    sums[52:53, :] = jnp.sum(flow * full, 0, keepdims=True)
    sums[53:57, :] = bias[...]
    block_out[...] = (
        (flat(feature[...].astype(F4)) + scale[...] * full).astype(BF).reshape(rows, cols, channels)
    )
    for r in range(rows + 6):
        wide[r, 0 : cols + 6, :] = padded[r].astype(F4)
    for j in range(7):
        total = [jnp.zeros((8, channels), F4) for _ in range(7)]
        for r in range(rows + 6):
            slab = wide[r, j : j + cols, :]
            for p in range(max(0, r - 6), min(rows, r + 1)):
                term = slab * grads[p]
                term = tree([term[8 * k : 8 * k + 8] for k in range(cols // 8)])
                total[r - p] = total[r - p] + term
        for i in range(7):
            sums[7 * i + j : 7 * i + j + 1, :] = jnp.sum(total[i], 0, keepdims=True)
    put_two(message, 0, sums[...])
    odd = index[0] != 0
    first, last = grads[0:3], grads[rows - 3 : rows]
    message[2 * SMALL : 2 * SMALL + 3 * cols, :] = (
        jnp.where(odd, first, last).astype(BF).reshape(3 * cols, channels)
    )
    outer[...] = jnp.where(odd, last, first).astype(BF)


def first_fan(index, win, wout, mine, theirs, one, three, two, shared):
    rows = win.shape[0] // 4
    shared[...] = (get_two(mine, 0) + get_two(theirs, 0)).astype(BF)
    for flip, message in ((1, one), (3, three), (2, two)):
        at = pl.multiple_of((index[1] ^ flip) * rows, rows)
        message[0:rows, :] = win[pl.ds(at, rows), :].astype(BF)
        message[rows : 2 * rows, :] = wout[pl.ds(at, rows), :].astype(BF)
        message[2 * rows :, :] = shared[...]


def second_fan(index, win, wout, mine, g1, g3, g2, total, one, three, two, shared):
    rows = win.shape[0] // 4
    at = pl.multiple_of(index[1] * rows, rows)
    for k, term in enumerate((win, wout)):
        own = term[pl.ds(at, rows), :]
        got = [g[k * rows : (k + 1) * rows, :].astype(F4) for g in (g1, g2, g3)]
        total[k] = tree([own] + got)
    small = tree([mine[...].astype(F4)] + [g[2 * rows :, :].astype(F4) for g in (g1, g2, g3)])
    shared[...] = small.astype(BF)
    part = rows // 4
    for flip, message in ((1, one), (3, three), (2, two)):
        at = pl.multiple_of((index[2] ^ flip) * part, part)
        for k in range(2):
            message[k * part : (k + 1) * part, :] = total[k, pl.ds(at, part), :].astype(BF)
        message[2 * part :, :] = shared[...]


def up16(n):
    return -(-n // 16) * 16


def send_half(total, k, bit, message):
    half = total.shape[1] // 2
    block = up16(half)
    value = jnp.where(bit, total[k, 0:half, :], total[k, half : 2 * half, :])
    message[k * block : k * block + half, :] = value.astype(BF)


def third_fan(index, before, mine, g1, g3, g2, total, message, shared):
    rows = before.shape[1] // 4
    at = pl.multiple_of(index[2] * rows, rows)
    for k in range(2):
        got = [g[k * rows : (k + 1) * rows, :].astype(F4) for g in (g1, g2, g3)]
        total[k] = tree([before[k, pl.ds(at, rows), :]] + got)
    small = tree([mine[...].astype(F4)] + [g[2 * rows :, :].astype(F4) for g in (g1, g2, g3)])
    put_two(shared, 0, small)
    held = message.shape[0] - 2 * SMALL
    for k in range(2):
        send_half(total, k, index[3] != 0, message)
    message[held:, :] = shared[...]


def quarter(ref, k, which):
    rows = ref.shape[1] // 4
    parts = [ref[k, i * rows : (i + 1) * rows, :] for i in range(4)]
    low = [jnp.where((which & 1) != 0, q, p) for p, q in (parts[:2], parts[2:])]
    return jnp.where((which & 2) != 0, low[1], low[0])


def fourth_fan(index, before, mine, got, total, two, one, three, shared):
    half = before.shape[1] // 2
    block = up16(half)
    bit = index[3] != 0
    for k in range(2):
        own = jnp.where(bit, before[k, half : 2 * half, :], before[k, 0:half, :])
        total[k] = own + got[k * block : k * block + half, :].astype(F4)
    shared[...] = (get_two(mine, 0) + get_two(got, 2 * block)).astype(BF)
    rows = half // 4
    block = up16(rows)
    for flip, message in ((1, one), (3, three), (2, two)):
        for k in range(2):
            message[k * block : k * block + rows, :] = quarter(total, k, index[4] ^ flip).astype(BF)
        message[2 * block :, :] = shared[...]


def last_sum(index, before, mine, g2, g1, g3, win, wout, small, bias):
    rows = before.shape[1] // 4
    block = up16(rows)
    for k, out in ((0, win), (1, wout)):
        got = [g[k * block : k * block + rows, :].astype(F4) for g in (g1, g2, g3)]
        out[...] = tree([quarter(before, k, index[4])] + got)
    total = tree([mine[...].astype(F4)] + [g[2 * block :, :].astype(F4) for g in (g1, g2, g3)])
    small[...] = total[0:53, :]
    wide = total.shape[1]
    for i in range(4):
        bias[i * wide : (i + 1) * wide] = total[53 + i]


def conv_back(index, tall, left, right, taps, cot, out, wide):
    rows, cols, channels = out.shape
    for r in range(rows + 6):
        wide[r, 8 : 8 + cols, :] = tall[r].astype(F4)
        wide[r, 5:8, :] = left[r].astype(F4)
        wide[r, 8 + cols : 11 + cols, :] = right[r].astype(F4)
    for lane in range(0, channels, 128):
        total = [cot[p, :, lane : lane + 128].astype(F4) for p in range(rows)]
        for j in range(7):
            weights = [taps[7 * i + j : 7 * i + j + 1, lane : lane + 128] for i in range(7)]
            for r in range(rows + 6):
                slab = wide[r, 11 - j : 11 - j + cols, lane : lane + 128]
                for p in range(max(0, r - 6), min(rows, r + 1)):
                    total[p] = total[p] + slab * weights[6 - (r - p)]
        for p in range(rows):
            out[p, :, lane : lane + 128] = total[p].astype(BF)


def tree(parts):
    while len(parts) > 1:
        parts = [p + q for p, q in zip(parts[::2], parts[1::2])]
    return parts[0]


def on_device(
    feature_map, kernel, ln_gain, ln_bias, w_in, b_in, w_out, b_out, layer_scale, cotangent
):
    row_count, col_count, channels = feature_map.shape
    pixels = row_count * col_count
    hidden_count = b_in.shape[0]
    contract_last = (((1,), (1,)), ((), ()))
    contract_first = (((0,), (0,)), ((), ()))

    weights = jnp.stack([w_in.T, w_out], 0)
    weights = quad_select(weights, "z", 2)
    weights = pair_gather(weights, "z", 1)
    rows = edges(feature_map, ROW, 0)
    weights, feature_map, cotangent, rows = lax.optimization_barrier(
        (weights, feature_map, cotangent, rows)
    )
    tall = between(feature_map, rows, 0)
    inner, outer = edge_sends(tall, COL, 1)
    outer_got = outer_swap(outer, COL)
    weights, inner_got = quad_gather(weights, Y, inner.reshape(-1, channels))
    columns = edge_order(inner_got.reshape(inner.shape), outer_got, COL)
    weights, tall, cotangent, kernel, ln_gain, layer_scale, b_out = lax.optimization_barrier(
        (weights, tall, cotangent, kernel, ln_gain, layer_scale, b_out)
    )
    weights = quad_gather(weights, "x")
    w_in_t, w_out_mine = weights[0], weights[1]
    core = lax.axis_index("c")
    half = hidden_count // 2
    z = lax.axis_index("z")
    units = hidden_count // 256
    b_order = (
        b_in.reshape(2, 2, 2, 2, 2, 4, 2, units).transpose(4, 5, 3, 6, 2, 0, 1, 7).reshape(hidden_count)
    )
    b_mine = lax.dynamic_slice_in_dim(b_order, core * half, half)
    grad_flow = cotangent.astype(F4).reshape(pixels, channels)
    grad_mixed = grad_flow * layer_scale

    taps = kernel.reshape(-1, channels)
    padded_low = between(tall, columns, 1)
    padded = padded_low.astype(F4)
    conv = jnp.zeros((row_count, col_count, channels), F4)
    for tap_row in range(7):
        for tap_col in range(7):
            conv = (
                conv
                + padded[tap_row : tap_row + row_count, tap_col : tap_col + col_count]
                * kernel[tap_row, tap_col]
            )
    average = jnp.mean(conv, -1, keepdims=True)
    centered = conv - average
    variance = jnp.mean(centered * centered, -1, keepdims=True)
    inv_std = lax.rsqrt(variance + 1e-06)
    unit_scaled = centered * inv_std
    normed = (unit_scaled * ln_gain + ln_bias).astype(BF).reshape(pixels, channels)
    ours = jnp.stack([normed, grad_mixed.astype(BF)], 0)
    theirs = swap(ours, "c", 1)
    normed_two = jnp.concatenate([ours[0], theirs[0]], 0)
    mixed_low = jnp.concatenate([ours[1], theirs[1]], 0)
    hidden = lax.dot_general(normed_two, w_in_t, contract_last, preferred_element_type=F4) + b_mine
    act_value, slope = gelu_parts(hidden)
    activated = act_value.astype(BF)
    grad_act = lax.dot_general(mixed_low, w_out_mine, contract_last, preferred_element_type=F4)
    grad_hidden = (grad_act * slope).astype(BF)
    grad_normed = jnp.dot(grad_hidden, w_in_t, preferred_element_type=F4)
    mixed = jnp.dot(activated, w_out_mine, preferred_element_type=F4)
    back = swap(jnp.stack([mixed[pixels:], grad_normed[pixels:]], 0).astype(BF), "c", 1)
    wout_term = lax.dot_general(activated, mixed_low, contract_first, preferred_element_type=F4)
    win_term = lax.dot_general(grad_hidden, normed_two, contract_first, preferred_element_type=F4)

    bias_mine = jnp.sum(grad_hidden.astype(F4), 0)
    bias_local = jnp.where(jnp.arange(2)[:, None] == core, bias_mine, 0.0)
    bias_local = (
        bias_local.reshape(2, 4, 2, 2, 2, 2, 2, units)
        .transpose(5, 6, 4, 2, 0, 1, 3, 7)
        .reshape(hidden_count // channels, channels)
    )
    index = jnp.stack(
        [core, lax.axis_index("x"), lax.axis_index(Y), z & 1, z // 2]
    ).astype(jnp.int32)
    grad_low, mine, outer, block_out = local_call(
        norm_back,
        index,
        [
            shape(row_count, col_count, channels, dtype=BF),
            shape(2 * SMALL + 3 * col_count, channels, dtype=BF),
            shape(3, col_count, channels, dtype=BF),
            shape(row_count, col_count, channels, dtype=BF),
        ],
        grad_normed, mixed, back, conv, ln_gain[None], padded_low, cotangent, feature_map,
        layer_scale[None], b_out[None], bias_local,
        scratch=[
            pltpu.VMEM((row_count, col_count, channels), F4),
            pltpu.VMEM((row_count + 6, col_count + 8, channels), F4),
            pltpu.VMEM((SMALL, channels), F4),
        ],
        flops=110 * pixels * channels,
    )
    theirs = swap(mine, "c", 1)
    small_shape = shape(SMALL, channels, dtype=BF)

    def message_of(rows, smalls=1):
        return shape(2 * rows + smalls * SMALL, channels, dtype=BF)

    def fan(messages, axis, flips, unit=1):
        return [swap(m, axis, flip * unit) for m, flip in zip(messages, flips)]

    piece = half // 4
    *messages, shared = local_call(
        first_fan, index, [message_of(piece)] * 3 + [small_shape], win_term, wout_term, mine, theirs
    )
    messages[2], outer = lax.optimization_barrier((messages[2], outer))
    got = fan(messages, "x", (1, 3, 2))
    outer_got = outer_swap(outer, ROW)
    rows = edge_order(theirs[2 * SMALL :].reshape(3, col_count, channels), outer_got, ROW)
    low_tall = between(grad_low, rows, 0)
    columns = edges(low_tall, COL, 1)
    total, *messages, shared = local_call(
        second_fan,
        index,
        [shape(2, piece, channels)] + [message_of(piece // 4)] * 3 + [small_shape],
        win_term, wout_term, shared, *got,
    )
    piece = piece // 4
    got = fan(messages, Y, (1, 3, 2))
    total, message, shared = local_call(
        third_fan,
        index,
        [
            shape(2, piece, channels),
            message_of(up16(piece // 2), 2),
            shape(2 * SMALL, channels, dtype=BF),
        ],
        total, shared, *got,
    )
    piece = piece // 2
    got = swap(message, "z", 1)
    total, *messages, shared = local_call(
        fourth_fan,
        index,
        [shape(2, piece, channels)] + [message_of(up16(units))] * 3 + [small_shape],
        total, shared, got,
    )
    got = fan(messages, "z", (2, 1, 3), 2)
    win_t, grad_w_out, small_grads, grad_b_in = local_call(
        last_sum,
        index,
        [shape(units, channels), shape(units, channels), shape(53, channels), shape(hidden_count)],
        total, shared, *got,
    )
    (grad_input,) = local_call(
        conv_back,
        index,
        [shape(row_count, col_count, channels, dtype=BF)],
        low_tall, *columns, taps, cotangent,
        scratch=[pltpu.VMEM((row_count + 6, col_count + 16, channels), F4)],
        flops=98 * pixels * channels,
    )
    return (block_out, grad_input, win_t.T, grad_w_out, small_grads, grad_b_in)


def solution(mesh):
    fine = Mesh(mesh.devices.reshape(8, 2, 2, 4, 2), ("z", "yh", "c", "x", "yl"))
    every = ROW + COL
    placed = (
        P(ROW, COL, None),
        P(),
        P(),
        P(),
        P(None, every),
        P(),
        P(every, None),
        P(),
        P(),
        P(ROW, COL, None),
    )
    return jax.shard_map(
        on_device,
        mesh=fine,
        in_specs=placed,
        out_specs=(
            P(ROW, COL, None),
            P(ROW, COL, None),
            P(None, every),
            P(every, None),
            P(),
            P(),
        ),
        check_vma=False,
    )
```
